128 devices in a mesh: st: 32 (over z, x, core), sb: 4 (over y).
Axes of the slice: x: 4, y: 4, z: 4, core: 2. Of those that a mesh axis runs over, the one named last changes fastest.
Arguments:
- volts: bfloat16 [2, 1024, 126976], P(None, 'st'), may hold values from -6 to 6
- prototype: float32 [16, 4096], replicated, may hold values from -1.5 to 1.5
- beam_channels: int32 [384], replicated, may hold values from 0 to 4095, as said below
- station_index: int32 [256], replicated, may hold values from 0 to 511, as said below
- delays: float32 [256, 256], replicated, may hold values from -64 to 64
- gains: float32 [256, 256], replicated, may hold values from 0.5 to 2
- assign: int32 [384, 1], replicated, may hold values from 0 to 3; in each aligned block of 384 rows (0 to 383, 384 to 767, ...) at most 160 rows name the same one
Outputs:
- visibility: float32 [2, 4, 32, 1024, 1024], P(None, 'sb', 'st')
- beam_out: float32 [4, 160, 2, 16, 512], P('sb', 'st')
The draws below stay inside these ranges and needn't reach their ends.
Inputs may be any that keep to these rules, and one draw needn't show every extreme that they name: `beam_channels`: 384 different channels. `station_index`: 256 different stations. `assign`: no index of sb receives more than 160 list entries, and some index receives exactly 160; every index receives at least one.
All inputs are finite; a program needn't handle non-finite values.
Results may differ from the reference program's by a relative error of at most 0.0054.
Values may be sent and summed in bfloat16 or wider, within the bound.
A program may use at most 192 MiB of HBM per device.

```python
import math
import jax
import jax.numpy as jnp
import numpy as np
from jax import lax

NCH = 4096
STATIONS = 512
TAPS = 16
FRAMES = 16
BEAMS = 256
BST = 256
BEAM_CH = 384
SLOTS = 160
SIGNALS = 1024
SAMPLES = 126976
CH_X = 32
N_ST = 32
N_SB = 4


def draw_beam_channels(key, part):
    return jax.random.permutation(jax.random.fold_in(key, 17), NCH)[:BEAM_CH].astype(jnp.int32)


def draw_station_index(key, part):
    return jax.random.permutation(jax.random.fold_in(key, 29), STATIONS)[:BST].astype(jnp.int32)


def level_of(stream_key, extent, cuts, low, largest):
    def one(dim, blocks):
        draws = jax.random.uniform(jax.random.fold_in(jax.random.fold_in(stream_key, 6), dim), (blocks,), jnp.float32, low / len(cuts), largest / len(cuts))
        return jnp.repeat(jnp.exp(draws), extent[dim] // blocks).reshape((-1,) + (1,) * (len(extent) - dim - 1))

    level = one(*cuts[0])
    for cut in cuts[1:]:
        level = level * one(*cut)
    return level


def shared_out(stream_key, own, number, rows, amount, top, bound, skew):
    sequence = jax.random.permutation(stream_key, amount)
    heavy_load, usual = load_shares(amount, rows * top, bound, skew, True), load_shares(amount, rows * top, bound, skew, False)
    places = jnp.arange(amount)

    def named(lengths, rotation):
        used = int((lengths > 0).sum())
        fixed = max(1, used // 4)
        passed = fixed + (places - fixed + rotation * (used - fixed)) % max(1, amount - fixed)
        return jnp.zeros((amount,), jnp.int32).at[sequence[jnp.where(places < fixed, places, passed)]].set(jnp.asarray(lengths, jnp.int32))

    lengths = jnp.where(number % 4 == 0, named(heavy_load, number // 4), named(usual, number - number // 4 - 1))
    mixed = jax.random.permutation(jax.random.fold_in(own, 3), amount)
    source_of, receiver = mixed[0:amount // 2 * 2:2], mixed[1:amount // 2 * 2:2]
    margin = jnp.minimum(lengths[source_of] - 1, bound - lengths[receiver]) // 2
    margin = jnp.where((source_of == sequence[0]) | (receiver == sequence[0]) | (lengths[receiver] == 0), 0, jnp.maximum(margin, 0))
    passed = jax.random.randint(jax.random.fold_in(own, 4), (amount // 2,), 0, 1 << 20) % (margin + 1)
    lengths = lengths.at[source_of].add(-passed).at[receiver].add(passed)
    labels = jnp.searchsorted(jnp.cumsum(lengths), jnp.arange(rows * top), side="right").astype(jnp.int32)
    grid = labels.reshape(top, rows).T
    grid = grid[jax.random.permutation(jax.random.fold_in(own, 1), rows)]
    rotation = jax.random.randint(jax.random.fold_in(own, 2), (rows, 1), 0, top)
    return jnp.take_along_axis(grid, (jnp.arange(top)[None, :] + rotation) % top, axis=1)


def load_shares(amount, total, most, lean, full):
    loads = [(1 << 20) // math.isqrt(standing ** lean) + 1 for standing in range(1, amount + 1)]
    largest = most if full else min(most, max(-(-total // amount), total * loads[0] // sum(loads)))
    least = 1 if total - largest >= amount - 1 else 0
    holding, rest = [largest] + [least] * (amount - 1), total - largest - least * (amount - 1)
    while rest > 0:
        movable = [i for i in range(1, amount) if holding[i] < largest] or [i for i in range(1, amount) if holding[i] < most]
        whole, remaining = sum([loads[i] for i in movable]), rest
        for i in movable:
            more = min(most - holding[i], max(1, remaining * loads[i] // whole), rest)
            holding[i] = holding[i] + more
            rest = rest - more
    return np.array(holding)


def scatter_about(key, dims, deviation, reach, shards=(), kind=jnp.bfloat16):
    array = jax.random.normal(key, dims, jnp.float32) * deviation
    if len(shards) > 0:
        array = level_of(key, dims, shards, -0.22, 0.18) * array
    return jnp.clip(array, min=-reach, max=reach).astype(kind)


def setup_inputs(seed: int = 0) -> dict:
    seeds = jax.random.split(jax.random.key(seed), 8)
    volts = scatter_about(seeds[0], (2, SIGNALS, SAMPLES), 1.0, 6.0, ((1, 32),))
    prototype = scatter_about(seeds[1], (TAPS, NCH), 0.25, 1.5, (), jnp.float32)
    beam_channels = draw_beam_channels(jax.random.fold_in(seeds[7], 71), 0)
    station_index = draw_station_index(jax.random.fold_in(seeds[7], 71), 0)
    delays = jnp.clip(jax.random.uniform(seeds[4], (BEAMS, BST), jnp.float32, -64.0, 64.0), -64.0, 64.0)
    gains = jnp.clip(jnp.exp(jax.random.uniform(seeds[5], (BEAMS, BST), jnp.float32, math.log(0.5), math.log(2.0))), 0.5, 2.0)
    assign_keys = jax.random.split(jax.random.fold_in(seeds[6], 1), BEAM_CH // BEAM_CH)
    assign_turns = jax.random.permutation(jax.random.fold_in(seeds[6], 3), BEAM_CH // BEAM_CH)
    assign = jax.vmap(lambda own, number: shared_out(jax.random.fold_in(seeds[6], 2), own, number, BEAM_CH, N_SB, 1, SLOTS, 2))(assign_keys, assign_turns).reshape((BEAM_CH, 1))
    return dict(volts=volts, prototype=prototype, beam_channels=beam_channels, station_index=station_index, delays=delays, gains=gains, assign=assign)


TWO_PI = 2.0 * math.pi

def polyphase(volts, prototype, frame_count):
    tap_count = prototype.shape[0]
    length = prototype.shape[1]
    segments = volts.reshape(2, volts.shape[1], frame_count + tap_count - 1, length)
    summed = jnp.zeros((2, volts.shape[1], frame_count, length), jnp.float32)
    for tap_idx in range(tap_count):
        summed = summed + prototype[tap_idx] * segments[:, :, tap_idx:tap_idx + frame_count, :].astype(jnp.float32)
    return summed.astype(jnp.bfloat16)

def dft_tables(channels, length):
    sample_ids = jnp.arange(length, dtype=jnp.int32)
    phase_ids = sample_ids[:, None] * channels[None, :].astype(jnp.int32) % length
    angles = phase_ids.astype(jnp.float32) * (TWO_PI / length)
    scale_dft = 1.0 / math.sqrt(length)
    return ((jnp.cos(angles) * scale_dft).astype(jnp.bfloat16), (jnp.sin(angles) * scale_dft).astype(jnp.bfloat16))

def transform(flat_rows, cos_t, sin_t):
    real_part = jnp.dot(flat_rows[0], cos_t, preferred_element_type=jnp.float32) + jnp.dot(flat_rows[1], sin_t, preferred_element_type=jnp.float32)
    imag_part = jnp.dot(flat_rows[1], cos_t, preferred_element_type=jnp.float32) - jnp.dot(flat_rows[0], sin_t, preferred_element_type=jnp.float32)
    return jnp.stack([real_part, imag_part]).astype(jnp.bfloat16)

def correlate(grouped):
    stacked = jnp.concatenate([grouped[0], grouped[1]], axis=1)
    turned = jnp.concatenate([grouped[1], -grouped[0]], axis=1)
    inverse = 1.0 / grouped.shape[2]
    vis_re = jnp.dot(stacked, stacked.T, preferred_element_type=jnp.float32) * inverse
    vis_im = jnp.dot(turned, stacked.T, preferred_element_type=jnp.float32) * inverse
    return jnp.stack([vis_re, vis_im])

def beam_weights(delays, gains, channel, length, listed):
    angles = delays * (channel.astype(jnp.float32) * (TWO_PI / length))
    scaling = gains * (1.0 / math.sqrt(listed))
    return ((scaling * jnp.cos(angles)).astype(jnp.bfloat16), (-scaling * jnp.sin(angles)).astype(jnp.bfloat16))

def combine(spectrum, w_re, w_im):
    real_in = spectrum[:, 0]
    imag_in = spectrum[:, 1]

    def product(operand, weight):
        return jnp.einsum('sfjp,sbj->sfpb', operand, weight, preferred_element_type=jnp.float32)
    out_re = product(real_in, w_re) - product(imag_in, w_im)
    out_im = product(imag_in, w_re) + product(real_in, w_im)
    stacked = jnp.stack([out_re, out_im], axis=1)
    return stacked.reshape(stacked.shape[0], 2, stacked.shape[2], -1)

def reference(volts, prototype, beam_channels, station_index, delays, gains, assign):
    signals = volts.shape[1]
    filtered = polyphase(volts, prototype, FRAMES)
    flat_rows = filtered.reshape(2, signals * FRAMES, NCH)
    cos_t, sin_t = dft_tables(jnp.arange(NCH, dtype=jnp.int32), NCH)
    spectra = transform(flat_rows, cos_t, sin_t).reshape(2, signals, FRAMES, NCH)
    groups = NCH // CH_X
    grouped = jnp.moveaxis(spectra.reshape(2, signals, FRAMES, groups, CH_X), 3, 0).reshape(groups, 2, signals, FRAMES * CH_X)
    visibility = lax.map(correlate, grouped)
    visibility = jnp.moveaxis(visibility, 1, 0).reshape(2, N_SB, N_ST, signals, signals)
    chosen = jnp.moveaxis(jnp.take(spectra, beam_channels, axis=3), 3, 0)
    listed = station_index.shape[0]

    def one_entry(packed):
        spectrum, channel = packed
        stations = jnp.swapaxes(spectrum, 1, 2).reshape(1, 2, FRAMES, signals // 2, 2)
        picked = jnp.take(stations, station_index, axis=3)
        w_re, w_im = beam_weights(delays[None], gains[None], channel.reshape(1, 1, 1), NCH, listed)
        return combine(picked.astype(jnp.float32), w_re.astype(jnp.float32), w_im.astype(jnp.float32))[0]
    entries = lax.map(one_entry, (chosen, beam_channels))
    owners = assign[:, 0]
    order = jnp.arange(BEAM_CH, dtype=jnp.int32)
    earlier = (owners[:, None] == owners[None, :]) & (order[None, :] < order[:, None])
    position = lax.optimization_barrier(jnp.sum(earlier.astype(jnp.int32), axis=1))
    beam_out = jnp.zeros((N_SB, SLOTS, 2, FRAMES, 2 * BEAMS), jnp.float32).at[owners, position].set(entries)
    return (visibility, beam_out)
```

```python
import math

import jax
import jax.numpy as jnp
from jax import lax
from jax.sharding import PartitionSpec as P

NCH = 4096
FRAMES = 16
SLOTS = 160


TWO_PI = 2.0 * math.pi


def polyphase(volts, prototype, frame_count):
    tap_count = prototype.shape[0]
    length = prototype.shape[1]
    segments = volts.reshape(2, volts.shape[1], frame_count + tap_count - 1, length)
    summed = jnp.zeros((2, volts.shape[1], frame_count, length), jnp.float32)
    for tap_idx in range(tap_count):
        summed = summed + prototype[tap_idx] * segments[
            :, :, tap_idx : tap_idx + frame_count, :
        ].astype(jnp.float32)
    return summed.astype(jnp.bfloat16)


def dft_tables(channels, length):
    sample_ids = jnp.arange(length, dtype=jnp.int32)
    phase_ids = sample_ids[:, None] * channels[None, :] % length
    angles = phase_ids.astype(jnp.float32) * (TWO_PI / length)
    scale_dft = 1.0 / math.sqrt(length)
    return (
        (jnp.cos(angles) * scale_dft).astype(jnp.bfloat16),
        (jnp.sin(angles) * scale_dft).astype(jnp.bfloat16),
    )


def transform(flat_rows, cos_t, sin_t):
    real_part = jnp.dot(flat_rows[0], cos_t, preferred_element_type=jnp.float32) + jnp.dot(
        flat_rows[1], sin_t, preferred_element_type=jnp.float32
    )
    imag_part = jnp.dot(flat_rows[1], cos_t, preferred_element_type=jnp.float32) - jnp.dot(
        flat_rows[0], sin_t, preferred_element_type=jnp.float32
    )
    return jnp.stack([real_part, imag_part]).astype(jnp.bfloat16)


def correlate(grouped):
    stacked = jnp.concatenate([grouped[0], grouped[1]], axis=1)
    turned = jnp.concatenate([grouped[1], -grouped[0]], axis=1)
    inverse = 1.0 / grouped.shape[2]
    vis_re = jnp.dot(stacked, stacked.T, preferred_element_type=jnp.float32) * inverse
    vis_im = jnp.dot(turned, stacked.T, preferred_element_type=jnp.float32) * inverse
    return jnp.stack([vis_re, vis_im])


def beam_weights(delays, gains, channel, length, listed):
    angles = delays * (channel.astype(jnp.float32) * (TWO_PI / length))
    scaling = gains * (1.0 / math.sqrt(listed))
    return (
        (scaling * jnp.cos(angles)).astype(jnp.bfloat16),
        (-scaling * jnp.sin(angles)).astype(jnp.bfloat16),
    )


def combine(spectrum, w_re, w_im):
    real_in = spectrum[:, 0]
    imag_in = spectrum[:, 1]

    def product(operand, weight):
        return jnp.einsum("sfjp,sbj->sfpb", operand, weight, preferred_element_type=jnp.float32)

    out_re = product(real_in, w_re) - product(imag_in, w_im)
    out_im = product(imag_in, w_re) + product(real_in, w_im)
    stacked = jnp.stack([out_re, out_im], axis=1)
    return stacked.reshape(stacked.shape[0], 2, stacked.shape[2], -1)


def body(volts, prototype, beam_channels, station_index, delays, gains, assign):
    sig_dev = volts.shape[1]
    st_count = lax.axis_size("st")
    sb_count = lax.axis_size("sb")
    sb_here = lax.axis_index("sb")
    st_here = lax.axis_index("st")
    filtered = polyphase(volts, prototype, FRAMES)
    flat_rows = filtered.reshape(2, sig_dev * FRAMES, NCH)
    band_width = NCH // sb_count
    channels = sb_here * band_width + jnp.arange(band_width, dtype=jnp.int32)
    cos_t, sin_t = dft_tables(channels, NCH)
    spectra = transform(flat_rows, cos_t, sin_t).reshape(2, sig_dev, FRAMES, band_width)
    turned_over = lax.all_to_all(spectra, "st", split_axis=3, concat_axis=1, tiled=True)
    signals = turned_over.shape[1]
    visibility = correlate(turned_over.reshape(2, signals, -1)).reshape(2, 1, 1, signals, signals)
    owners = assign[:, 0]
    matches = (owners == sb_here).astype(jnp.int32)
    order = jnp.arange(matches.shape[0], dtype=jnp.int32)
    earlier = (order[None, :] < order[:, None]).astype(jnp.int32)
    position = jnp.sum(earlier * matches[None, :], axis=1)
    slot_ids = jnp.arange(SLOTS, dtype=jnp.int32)
    picker = matches[None, :] * (position[None, :] == slot_ids[:, None]).astype(jnp.int32)
    filled = jnp.sum(picker, axis=1)
    slot_channel = jnp.sum(picker * beam_channels[None, :], axis=1)
    per_dev = SLOTS // st_count
    listed = station_index.shape[0]
    cos_b, sin_b = dft_tables(slot_channel, NCH)
    slot_spectra = transform(flat_rows, cos_b, sin_b) * filled.astype(jnp.bfloat16)[None, None, :]
    slot_spectra = slot_spectra.reshape(2, sig_dev, FRAMES, SLOTS).transpose(3, 0, 2, 1)
    stations_dev = sig_dev // 2
    local_ids = st_here * stations_dev + jnp.arange(stations_dev, dtype=jnp.int32)
    chooser = (station_index[:, None] == local_ids[None, :]).astype(jnp.float32)
    delay_local = jnp.sum(delays[:, :, None] * chooser[None, :, :], axis=1)
    gain_local = jnp.sum(gains[:, :, None] * chooser[None, :, :], axis=1)
    spectrum = slot_spectra.reshape(per_dev * lax.axis_size("st"), 2, FRAMES, stations_dev, 2)
    w_re, w_im = beam_weights(
        delay_local[None], gain_local[None], slot_channel[:, None, None], NCH, listed
    )
    beam_out = lax.psum_scatter(
        combine(spectrum, w_re, w_im), "st", scatter_dimension=0, tiled=True
    )
    beam_out = beam_out.reshape(1, per_dev, 2, FRAMES, -1)
    return (visibility, beam_out)


def solution(mesh):
    in_specs = (P(None, "st", None), P(), P(), P(), P(), P(), P())
    out_specs = (P(None, "sb", "st", None, None), P("sb", "st", None, None, None))
    return jax.shard_map(body, mesh=mesh, in_specs=in_specs, out_specs=out_specs, check_vma=False)
```

```python
import math

import jax
import jax.numpy as jnp
from jax import lax
from jax.experimental import pallas as pl
from jax.experimental.pallas import tpu as pltpu
from jax.sharding import PartitionSpec as P

NCH = 4096
FRAMES = 16
TAPS = 16
SLOTS = 160
BAND = 1024
GROUPS = 32
PER_DEV = 5
QUARTER = 1024
SIG = 16
SIGNALS = 1024
ROWS = 80
NT = (((1,), (1,)), ((), ()))
F32 = jnp.float32
BF16 = jnp.bfloat16
VMEM_LIMIT = 56 << 20
MESH = pl.DeviceIdType.MESH
PIECES = ((0, 32), (32, 16), (48, 16), (64, 16))


def sincos_turns(turns):
    quarter = jnp.floor(turns * 4.0 + 0.5)
    x = (turns - quarter * 0.25) * (2.0 * math.pi)
    z = x * x
    sin_x = x * (1.0 + z * (-1.0 / 6 + z * (1.0 / 120 + z * (-1.0 / 5040 + z * (1.0 / 362880)))))
    cos_x = 1.0 + z * (-0.5 + z * (1.0 / 24 + z * (-1.0 / 720 + z * (1.0 / 40320))))
    which = quarter.astype(jnp.int32) & 3
    odd = (which & 1) == 1
    s = jnp.where(odd, cos_x, sin_x)
    c = jnp.where(odd, sin_x, cos_x)
    s = jnp.where(which >= 2, -s, s)
    c = jnp.where((which == 1) | (which == 2), -c, c)
    return s, c


def fill_tables(chan_ref, table):
    @pl.loop(0, chan_ref.shape[0] // 32)
    def _(block):
        at = pl.ds(pl.multiple_of(block * 32, 32), 32)
        wide = jnp.broadcast_to(chan_ref[at, :], (32, 128))
        lane = lax.broadcasted_iota(jnp.int32, (32, 128), 1)
        s, c = sincos_turns(((lane * wide) & (NCH - 1)).astype(F32) * (1.0 / NCH))
        s_step, c_step = sincos_turns(((128 * wide) & (NCH - 1)).astype(F32) * (1.0 / NCH))
        s, c = s * (1.0 / 64), c * (1.0 / 64)
        for tile in range(QUARTER // 128):
            lanes = slice(tile * 128, tile * 128 + 128)
            table[0, at, lanes] = c.astype(BF16)
            table[1, at, lanes] = s.astype(BF16)
            s, c = s * c_step + c * s_step, c * c_step - s * s_step


def filter_group(volts, proto_ref, filt, spec):
    @pl.loop(0, QUARTER // 128)
    def _(tile):
        @pl.loop(0, 4)
        def _(n1):
            base = pl.multiple_of(n1 * QUARTER + tile * 128, 128)
            taps = [
                jnp.broadcast_to(proto_ref[t : t + 1, pl.ds(base, 128)], (SIG, 128))
                for t in range(TAPS)
            ]
            for part in range(2):
                for half in range(2):
                    acc = [None] * 8
                    for u in range(8 + TAPS - 1):
                        at = pl.multiple_of((half * 8 + u) * NCH + base, 128)
                        v = volts[part, :, pl.ds(at, 128)].astype(F32)
                        for f in range(8):
                            t = u - f
                            if 0 <= t < TAPS:
                                term = taps[t] * v
                                acc[f] = term if acc[f] is None else acc[f] + term
                    for f in range(8):
                        filt[part * 4 + n1, half * 8 + f] = acc[f]

        lanes = pl.ds(pl.multiple_of(tile * 128, 128), 128)
        for f in range(FRAMES):
            re = [filt[n1, f] for n1 in range(4)]
            im = [filt[4 + n1, f] for n1 in range(4)]
            ar, ai = re[0] + re[2], im[0] + im[2]
            br, bi = re[0] - re[2], im[0] - im[2]
            cr, ci = re[1] + re[3], im[1] + im[3]
            dr, di = re[1] - re[3], im[1] - im[3]
            outs = [(ar + cr, ai + ci), (br + di, bi - dr), (ar - cr, ai - ci), (br - di, bi + dr)]
            for k1 in range(4):
                for part in range(2):
                    at = part * 256 + f * SIG
                    spec[k1, at : at + SIG, lanes] = outs[k1][part].astype(BF16)


def by_group(re, im):
    joined = jnp.concatenate([re.reshape(32, 8, 256), im.reshape(32, 8, 256)], axis=1)
    return joined.astype(BF16)


def exchange_kernel(
    volts_hbm, proto_ref, chan_ref, recv_ref,
    volts, table, filt, spec, send, load_sem, own_sem, send_sem, recv_sem,
):
    n = GROUPS
    me = lax.axis_index("st")

    def load(g):
        src = volts_hbm.at[:, pl.ds(g * SIG, SIG), :]
        return pltpu.make_async_copy(src, volts.at[g], load_sem.at[g])

    load(0).start()
    load(1).start()
    barrier = pltpu.get_barrier_semaphore()

    @pl.loop(1, n)
    def _(d):
        there = lax.rem(me + d, n)
        pl.semaphore_signal(barrier, inc=1, device_id={"st": there}, device_id_type=MESH)

    fill_tables(chan_ref, table)
    pl.semaphore_wait(barrier, n - 1)

    def own(g):
        return pltpu.make_async_copy(send.at[g, me], recv_ref.at[g, me], own_sem.at[g])

    def remote(g, piece, there):
        rows = pl.ds(*PIECES[piece])
        return pltpu.make_async_remote_copy(
            src_ref=send.at[g, there, rows],
            dst_ref=recv_ref.at[g, me, rows],
            send_sem=send_sem.at[g, piece],
            recv_sem=recv_sem.at[g, piece],
            device_id={"st": there},
            device_id_type=MESH,
        )

    def start(g, piece):
        @pl.loop(1, n)
        def _(d):
            remote(g, piece, lax.rem(me + d, n)).start()

    @pl.loop(0, 2)
    def _(g):
        src = volts_hbm.at[:, pl.ds(g * SIG, SIG), :]
        pltpu.make_async_copy(src, volts.at[g], load_sem.at[g]).wait()
        filter_group(volts.at[g], proto_ref, filt, spec)

        def both(k1, rows):
            a = spec[k1]
            c = lax.dot_general(table[0, rows], a, NT, preferred_element_type=F32)
            s = lax.dot_general(table[1, rows], a, NT, preferred_element_type=F32)
            return c[:, :256] + s[:, 256:], c[:, 256:] - s[:, :256]

        chan = chan_ref[1024:1280, :]
        beam_re = jnp.zeros((256, 256), F32)
        beam_im = jnp.zeros((256, 256), F32)
        for k1 in range(4):
            re, im = both(k1, slice(1024, 1280))
            mine = (chan & 3) == k1
            beam_re = jnp.where(mine, re, beam_re)
            beam_im = jnp.where(mine, im, beam_im)
        row = lax.broadcasted_iota(jnp.int32, (256, 256), 0)
        col = lax.broadcasted_iota(jnp.int32, (256, 256), 1)
        turn = (row == (col & 15) * 16 + (col >> 4)).astype(F32).astype(BF16)
        joined = by_group(beam_re, beam_im).reshape(512, 256)
        turned = jnp.dot(joined, turn, preferred_element_type=F32)
        send[g, :, 0:16, :] = turned.astype(BF16).reshape(32, 16, 256)
        for k1 in range(4):
            re, im = both(k1, slice(k1 * 256, k1 * 256 + 256))
            send[g, :, 16 + k1 * 16 : 32 + k1 * 16, :] = by_group(re, im)
            start(g, k1)
        own(g).start()

    for g in range(2):
        own(g).wait()
        for piece in range(4):
            rows = pl.ds(*PIECES[piece])
            others = pl.ds(0, n - 1)
            all_of = pltpu.make_async_remote_copy(
                src_ref=send.at[g, others, rows],
                dst_ref=recv_ref.at[g, others, rows],
                send_sem=send_sem.at[g, piece],
                recv_sem=recv_sem.at[g, piece],
                device_id={"st": lax.rem(me + 1, n)},
                device_id_type=MESH,
            )
            all_of.wait_send()
            all_of.wait_recv()


def exchange(volts, prototype, chan):
    vmem = pl.BlockSpec(memory_space=pltpu.VMEM)
    hbm = pl.BlockSpec(memory_space=pl.ANY)
    return pl.pallas_call(
        exchange_kernel,
        out_shape=jax.ShapeDtypeStruct((2, GROUPS, ROWS, 256), BF16),
        in_specs=[hbm, vmem, vmem],
        out_specs=hbm,
        scratch_shapes=[
            pltpu.VMEM((2, 2, SIG, volts.shape[2]), BF16),
            pltpu.VMEM((2, chan.shape[0], QUARTER), BF16),
            pltpu.VMEM((8, FRAMES, SIG, 128), F32),
            pltpu.VMEM((4, 512, QUARTER), BF16),
            pltpu.VMEM((2, GROUPS, ROWS, 256), BF16),
            pltpu.SemaphoreType.DMA((2,)),
            pltpu.SemaphoreType.DMA((2,)),
            pltpu.SemaphoreType.DMA((2, 4)),
            pltpu.SemaphoreType.DMA((2, 4)),
        ],
        compiler_params=pltpu.CompilerParams(
            vmem_limit_bytes=VMEM_LIMIT, collective_id=0, has_side_effects=True
        ),
        name="channelise",
    )(volts, prototype, chan)


def correlate_kernel(recv_ref, out_ref, plain, turned):
    @pl.when(pl.program_id(0) == 0)
    def _():
        @pl.loop(0, 32)
        def _(src):
            for chunk in range(2):
                block = recv_ref[chunk, src, 16:80, :].astype(F32)
                parts = [block[:, :128], block[:, 128:]]
                stacked = jnp.concatenate(parts, axis=0)
                by_part = stacked.reshape(8, 2, 8, 128)
                swapped = jnp.stack([by_part[:, 1], -by_part[:, 0]], axis=1).reshape(128, 128)
                at = pl.ds(pl.multiple_of(src * 32 + chunk * SIG, SIG), SIG)
                for x, dest in ((stacked, plain), (swapped, turned)):
                    t = x.T.astype(BF16)
                    for f in range(8):
                        dest[at, f * 128 : f * 128 + 128] = t[f * 16 : f * 16 + 16]

    rows = pl.ds(pl.multiple_of(pl.program_id(0) * 256, 256), 256)
    whole = plain[...]
    scale = 1.0 / 512
    out_ref[0, 0, 0] = lax.dot_general(plain[rows, :], whole, NT, preferred_element_type=F32) * scale
    out_ref[1, 0, 0] = lax.dot_general(turned[rows, :], whole, NT, preferred_element_type=F32) * scale


def correlate(recv):
    once = pl.Buffered(1)
    whole = pl.BlockSpec((2, GROUPS, ROWS, 256), lambda i: (0, 0, 0, 0), pipeline_mode=once)
    return pl.pallas_call(
        correlate_kernel,
        grid=(4,),
        out_shape=jax.ShapeDtypeStruct((2, 1, 1, SIGNALS, SIGNALS), F32),
        in_specs=[whole],
        out_specs=pl.BlockSpec((2, 1, 1, 256, SIGNALS), lambda i: (0, 0, 0, i, 0)),
        scratch_shapes=[pltpu.VMEM((SIGNALS, 1024), BF16), pltpu.VMEM((SIGNALS, 1024), BF16)],
        compiler_params=pltpu.CompilerParams(vmem_limit_bytes=VMEM_LIMIT),
        name="correlate",
    )(recv)


def beams_kernel(x_ref, station_ref, delay_ref, gain_ref, chan_ref, filled_ref, out_ref):
    listed = station_ref.shape[1]
    row = lax.broadcasted_iota(jnp.int32, (512, listed), 0)
    station = (row & 31) * 16 + ((row >> 5) & 1) * 8 + (row >> 6)
    select = (station == station_ref[...]).astype(F32).astype(BF16)
    x = []
    for r in range(2 * PER_DEV):
        t = x_ref[r].astype(F32).T.astype(BF16)
        x.append(jnp.concatenate([t[s * 32 : s * 32 + 32] for s in range(8)], axis=1))
    picked = jnp.dot(jnp.concatenate(x, axis=0), select, preferred_element_type=F32).astype(BF16)
    scaling = gain_ref[...] * (1.0 / math.sqrt(listed))
    for slot in range(PER_DEV):
        turns = delay_ref[...] * (chan_ref[0, slot].astype(F32) * (1.0 / NCH))
        turns = turns - jnp.floor(turns)
        s, c = sincos_turns(turns)
        level = scaling * filled_ref[0, slot].astype(F32)
        w_re, w_im = (level * c).astype(BF16), (-level * s).astype(BF16)
        at = slot * 64
        pair = picked[at : at + 64]
        with_re = lax.dot_general(pair, w_re, NT, preferred_element_type=F32)
        with_im = lax.dot_general(pair, w_im, NT, preferred_element_type=F32)
        out_re = with_re[:32] - with_im[32:]
        out_im = with_re[32:] + with_im[:32]
        for part, out in enumerate((out_re, out_im)):
            out_ref[0, slot, part, :, 0:256] = out[:16]
            out_ref[0, slot, part, :, 256:512] = out[16:]


def beams(x, station_index, delays, gains, chan, filled):
    smem = pl.BlockSpec(memory_space=pltpu.SMEM)
    vmem = pl.BlockSpec(memory_space=pltpu.VMEM)
    return pl.pallas_call(
        beams_kernel,
        out_shape=jax.ShapeDtypeStruct((1, PER_DEV, 2, FRAMES, 512), F32),
        in_specs=[vmem, vmem, vmem, vmem, smem, smem],
        out_specs=vmem,
        compiler_params=pltpu.CompilerParams(vmem_limit_bytes=VMEM_LIMIT),
        name="beams",
    )(x, station_index, delays, gains, chan, filled)


def body(volts, prototype, beam_channels, station_index, delays, gains, assign):
    sb_here = lax.axis_index("sb")
    st_here = lax.axis_index("st")
    owners = assign[:, 0]
    order = jnp.arange(owners.shape[0], dtype=jnp.int32)
    matches = (owners == sb_here).astype(jnp.int32)
    position = jnp.sum((order[None, :] < order[:, None]).astype(jnp.int32) * matches[None, :], axis=1)
    row = jnp.arange(256, dtype=jnp.int32)
    slot = jnp.where((row & 7) < PER_DEV, (row >> 3) * PER_DEV + (row & 7), -1)
    picker = matches[None, :] * (position[None, :] == slot[:, None]).astype(jnp.int32)
    filled = jnp.sum(picker, axis=1)
    slot_channel = jnp.sum(picker * beam_channels[None, :], axis=1)
    line = jnp.arange(1024, dtype=jnp.int32)
    main = sb_here * BAND + (line & 255) * 4 + (line >> 8)
    recv = exchange(volts, prototype, jnp.concatenate([main, slot_channel])[:, None])
    visibility = correlate(recv)
    x = recv[:, :, 0:16].reshape(2, 32, 2, 8, 256)[:, :, :, :PER_DEV]
    x = x.transpose(3, 2, 0, 1, 4).reshape(2 * PER_DEV, 64, 256)
    mine = lax.dynamic_slice_in_dim(slot_channel, st_here * 8, 8)[None]
    there = lax.dynamic_slice_in_dim(filled, st_here * 8, 8)[None]
    beam_out = beams(x, station_index[None], delays, gains, mine, there)
    return (visibility, beam_out)


def solution(mesh):
    in_specs = (P(None, "st", None), P(), P(), P(), P(), P(), P())
    out_specs = (P(None, "sb", "st", None, None), P("sb", "st", None, None, None))
    return jax.shard_map(body, mesh=mesh, in_specs=in_specs, out_specs=out_specs, check_vma=False)
```

```python
import math

import jax
import jax.numpy as jnp
from jax import lax
from jax.experimental import pallas as pl
from jax.experimental.pallas import tpu as pltpu
from jax.sharding import PartitionSpec as P

NCH = 4096
FRAMES = 16
TAPS = 16
SLOTS = 160
BAND = 1024
GROUPS = 32
PER_DEV = 5
QUARTER = 1024
SIG = 16
SIGNALS = 1024
ROWS = 80
NT = (((1,), (1,)), ((), ()))
F32 = jnp.float32
BF16 = jnp.bfloat16
VMEM_LIMIT = 56 << 20
MESH = pl.DeviceIdType.MESH
PIECES = ((0, 48), (48, 32))
HALF = 8
CHIPS = ((2, 2), (1, 2), (2, 1), (3, 2), (2, 3), (0, 2), (2, 0), (1, 1), (3, 3), (1, 3), (3, 1), (0, 1), (3, 0), (0, 3), (1, 0))
ORDER = tuple((z, x, c) for z, x in CHIPS for c in range(2)) + ((0, 0, 1),)


def sincos_turns(turns):
    quarter = jnp.floor(turns * 4.0 + 0.5)
    x = (turns - quarter * 0.25) * (2.0 * math.pi)
    z = x * x
    sin_x = x * (1.0 + z * (-1.0 / 6 + z * (1.0 / 120 + z * (-1.0 / 5040 + z * (1.0 / 362880)))))
    cos_x = 1.0 + z * (-0.5 + z * (1.0 / 24 + z * (-1.0 / 720 + z * (1.0 / 40320))))
    which = quarter.astype(jnp.int32) & 3
    odd = (which & 1) == 1
    s = jnp.where(odd, cos_x, sin_x)
    c = jnp.where(odd, sin_x, cos_x)
    s = jnp.where(which >= 2, -s, s)
    c = jnp.where((which == 1) | (which == 2), -c, c)
    return s, c


def fill_tables(chan_ref, table):
    @pl.loop(0, chan_ref.shape[0] // 32)
    def _(block):
        at = pl.ds(pl.multiple_of(block * 32, 32), 32)
        wide = jnp.broadcast_to(chan_ref[at, :], (32, 128))
        lane = lax.broadcasted_iota(jnp.int32, (32, 128), 1)
        s, c = sincos_turns(((lane * wide) & (NCH - 1)).astype(F32) * (1.0 / NCH))
        s_step, c_step = sincos_turns(((128 * wide) & (NCH - 1)).astype(F32) * (1.0 / NCH))
        s, c = s * (1.0 / 64), c * (1.0 / 64)
        which = block // 8
        cos_at = pl.ds(pl.multiple_of((block % 8) * 32, 32), 32)
        sin_at = pl.ds(pl.multiple_of((block % 8) * 32 + 256, 32), 32)
        for tile in range(QUARTER // 128):
            lanes = slice(tile * 128, tile * 128 + 128)
            table[which, cos_at, lanes] = c.astype(BF16)
            table[which, sin_at, lanes] = s.astype(BF16)
            s, c = s * c_step + c * s_step, c * c_step - s * s_step


def filter_frames(volts, half, proto_ref, filt, spec):
    @pl.loop(0, QUARTER // 128)
    def _(tile):
        @pl.loop(0, 4)
        def _(n1):
            base = pl.multiple_of(n1 * QUARTER + tile * 128, 128)
            taps = [
                jnp.broadcast_to(proto_ref[t : t + 1, pl.ds(base, 128)], (SIG, 128))
                for t in range(TAPS)
            ]
            for part in range(2):
                acc = [None] * HALF
                for u in range(HALF + TAPS - 1):
                    at = pl.multiple_of((half * HALF + u) * NCH + base, 128)
                    v = volts[part, :, pl.ds(at, 128)].astype(F32)
                    for f in range(HALF):
                        t = u - f
                        if 0 <= t < TAPS:
                            term = taps[t] * v
                            acc[f] = term if acc[f] is None else acc[f] + term
                for f in range(HALF):
                    filt[part * 4 + n1, f] = acc[f]

        lanes = pl.ds(pl.multiple_of(tile * 128, 128), 128)
        for f in range(HALF):
            re = [filt[n1, f] for n1 in range(4)]
            im = [filt[4 + n1, f] for n1 in range(4)]
            ar, ai = re[0] + re[2], im[0] + im[2]
            br, bi = re[0] - re[2], im[0] - im[2]
            cr, ci = re[1] + re[3], im[1] + im[3]
            dr, di = re[1] - re[3], im[1] - im[3]
            outs = [(ar + cr, ai + ci), (br + di, bi - dr), (ar - cr, ai - ci), (br - di, bi + dr)]
            for k1 in range(4):
                for part in range(2):
                    at = part * 128 + f * SIG
                    spec[k1, at : at + SIG, lanes] = outs[k1][part].astype(BF16)


def by_group(re, im):
    joined = jnp.concatenate([re.reshape(32, 8, 128), im.reshape(32, 8, 128)], axis=1)
    return joined.astype(BF16)


def exchange_kernel(
    volts_hbm, proto_ref, chan_ref, delay_ref, gain_ref, mine_ref, filled_ref,
    plain_hbm, turned_hbm, beam_hbm, weight_hbm,
    volts, table, filt, spec, send, recv, plain, turned, weight,
    load_sem, own_sem, send_sem, recv_sem, out_sem,
):
    n = GROUPS
    me = lax.axis_index("st")

    def load(g):
        src = volts_hbm.at[:, pl.ds(g * SIG, SIG), :]
        return pltpu.make_async_copy(src, volts.at[g], load_sem.at[g])

    load(0).start()
    barrier = pltpu.get_barrier_semaphore()

    @pl.loop(1, n)
    def _(d):
        there = lax.rem(me + d, n)
        pl.semaphore_signal(barrier, inc=1, device_id={"st": there}, device_id_type=MESH)

    fill_tables(chan_ref, table)
    load(1).start()
    pl.semaphore_wait(barrier, n - 1)

    def own(q):
        return pltpu.make_async_copy(send.at[q, me], recv.at[q, me], own_sem.at[q])

    def remote(q, piece, there):
        rows = pl.ds(*PIECES[piece])
        return pltpu.make_async_remote_copy(
            src_ref=send.at[q, there, rows],
            dst_ref=recv.at[q, me, rows],
            send_sem=send_sem.at[q, piece],
            recv_sem=recv_sem.at[q, piece],
            device_id={"st": there},
            device_id_type=MESH,
        )

    def start(q, piece):
        plane, column, core = me // 8, (me // 2) % 4, me % 2
        for dz, dx, dc in ORDER:
            there = ((plane + dz) % 4) * 8 + ((column + dx) % 4) * 2 + (core + dc) % 2
            remote(q, piece, there).start()

    @pl.loop(0, 4)
    def _(step):
        g, half = step // 2, step % 2
        q = half * 2 + g

        @pl.when(half == 0)
        def _():
            src = volts_hbm.at[:, pl.ds(g * SIG, SIG), :]
            pltpu.make_async_copy(src, volts.at[g], load_sem.at[g]).wait()

        filter_frames(volts.at[g], half, proto_ref, filt, spec)

        def both(k1, which):
            t = lax.dot_general(table[which], spec[k1], NT, preferred_element_type=F32)
            c, s = t[:256], t[256:]
            return c[:, :128] + s[:, 128:], c[:, 128:] - s[:, :128]

        chan = chan_ref[1024:1280, :]
        beam_re = jnp.zeros((256, 128), F32)
        beam_im = jnp.zeros((256, 128), F32)
        for k1 in range(4):
            re, im = both(k1, 4)
            mine = (chan & 3) == k1
            beam_re = jnp.where(mine, re, beam_re)
            beam_im = jnp.where(mine, im, beam_im)
        row = lax.broadcasted_iota(jnp.int32, (128, 128), 0)
        col = lax.broadcasted_iota(jnp.int32, (128, 128), 1)
        turn = (row == (col & 7) * 16 + (col >> 3)).astype(F32).astype(BF16)
        joined = by_group(beam_re, beam_im).reshape(512, 128)
        placed = jnp.dot(joined, turn, preferred_element_type=F32)
        send[q, :, 0:16, :] = placed.astype(BF16).reshape(32, 16, 128)
        for k1 in range(4):
            re, im = both(k1, k1)
            send[q, :, 16 + k1 * 16 : 32 + k1 * 16, :] = by_group(re, im)
            if k1 % 2 == 1:
                start(q, k1 // 2)
        own(q).start()

    @pl.loop(0, delay_ref.shape[0] // 32)
    def _(block):
        at = pl.ds(pl.multiple_of(block * 32, 32), 32)
        scaling = gain_ref[at, :] * (1.0 / math.sqrt(gain_ref.shape[1]))
        for slot in range(PER_DEV):
            turns = delay_ref[at, :] * (mine_ref[0, slot].astype(F32) * (1.0 / NCH))
            turns = turns - jnp.floor(turns)
            s, c = sincos_turns(turns)
            level = scaling * filled_ref[0, slot].astype(F32)
            weight[slot, 0, at, :] = (level * c).astype(BF16)
            weight[slot, 1, at, :] = (-level * s).astype(BF16)

    copies = [pltpu.make_async_copy(weight, weight_hbm, out_sem.at[0])]
    copies[0].start()
    for g in range(2):
        for q in (g, 2 + g):
            own(q).wait()
            for piece in range(len(PIECES)):
                rows = pl.ds(*PIECES[piece])
                others = pl.ds(0, n - 1)
                all_of = pltpu.make_async_remote_copy(
                    src_ref=send.at[q, others, rows],
                    dst_ref=recv.at[q, others, rows],
                    send_sem=send_sem.at[q, piece],
                    recv_sem=recv_sem.at[q, piece],
                    device_id={"st": lax.rem(me + 1, n)},
                    device_id_type=MESH,
                )
                all_of.wait_send()
                all_of.wait_recv()
            beam = pltpu.make_async_copy(recv.at[q, :, 0:16], beam_hbm.at[q], out_sem.at[1 + q])
            beam.start()
            copies.append(beam)

        @pl.loop(0, n)
        def _(src):
            block = jnp.concatenate([recv[g, src, 16:80, :], recv[2 + g, src, 16:80, :]], axis=0)
            block = block.astype(F32)
            by_part = block.reshape(8, 2, 8, 128)
            swapped = jnp.stack([by_part[:, 1], -by_part[:, 0]], axis=1).reshape(128, 128)
            for x, dest in ((block, plain), (swapped, turned)):
                t = x.T.astype(BF16)
                for f in range(HALF):
                    dest[src, g, :, f * 128 : f * 128 + 128] = t[f * SIG : f * SIG + SIG]

        for i, (mem, out) in enumerate(((plain, plain_hbm), (turned, turned_hbm))):
            copy = pltpu.make_async_copy(mem.at[:, g], out.at[:, g], out_sem.at[5 + 2 * g + i])
            copy.start()
            copies.append(copy)
    for copy in copies:
        copy.wait()


def exchange(volts, prototype, chan, delays, gains, mine, filled):
    vmem = pl.BlockSpec(memory_space=pltpu.VMEM)
    smem = pl.BlockSpec(memory_space=pltpu.SMEM)
    hbm = pl.BlockSpec(memory_space=pl.ANY)
    blocks = (4, GROUPS, ROWS, 128)
    spectra = (GROUPS, 2, SIG, 1024)
    weight = (PER_DEV, 2) + delays.shape
    return pl.pallas_call(
        exchange_kernel,
        out_shape=[
            jax.ShapeDtypeStruct(spectra, BF16),
            jax.ShapeDtypeStruct(spectra, BF16),
            jax.ShapeDtypeStruct((4, GROUPS, 16, 128), BF16),
            jax.ShapeDtypeStruct(weight, BF16),
        ],
        in_specs=[hbm, vmem, vmem, vmem, vmem, smem, smem],
        out_specs=[hbm] * 4,
        scratch_shapes=[
            pltpu.VMEM((2, 2, SIG, volts.shape[2]), BF16),
            pltpu.VMEM((5, 512, QUARTER), BF16),
            pltpu.VMEM((8, HALF, SIG, 128), F32),
            pltpu.VMEM((4, 256, QUARTER), BF16),
            pltpu.VMEM(blocks, BF16),
            pltpu.VMEM(blocks, BF16),
            pltpu.VMEM(spectra, BF16),
            pltpu.VMEM(spectra, BF16),
            pltpu.VMEM(weight, BF16),
            pltpu.SemaphoreType.DMA((2,)),
            pltpu.SemaphoreType.DMA((4,)),
            pltpu.SemaphoreType.DMA((4, len(PIECES))),
            pltpu.SemaphoreType.DMA((4, len(PIECES))),
            pltpu.SemaphoreType.DMA((9,)),
        ],
        compiler_params=pltpu.CompilerParams(
            vmem_limit_bytes=VMEM_LIMIT, collective_id=0, has_side_effects=True
        ),
        name="exchange",
    )(volts, prototype, chan, delays, gains, mine, filled)


def correlate_kernel(plain_ref, turned_ref, beam_ref, weight_ref, station_ref, vis_ref, beam_out_ref, wide):
    @pl.when(pl.program_id(0) == 0)
    def _():
        listed = station_ref.shape[1]
        row = lax.broadcasted_iota(jnp.int32, (512, listed), 0)
        station = (row & 31) * 16 + ((row >> 5) & 1) * 8 + (row >> 6)
        select = (station == station_ref[...]).astype(F32).astype(BF16)
        wide[...] = beam_ref[...].reshape(4 * 512, 128).astype(F32)
        rows = []
        for slot in range(PER_DEV):
            for part in range(2):
                for half in range(2):
                    first = half * 1024 + part * 8 + slot
                    x = wide[pl.ds(first, 64, stride=16), :]
                    t = x.T.astype(BF16)
                    rows.append(jnp.concatenate([t[s * 16 : s * 16 + 16] for s in range(8)], axis=1))
        picked = jnp.dot(jnp.concatenate(rows, axis=0), select, preferred_element_type=F32).astype(BF16)
        for slot in range(PER_DEV):
            pair = picked[slot * 64 : slot * 64 + 64]
            with_re = lax.dot_general(pair, weight_ref[slot, 0], NT, preferred_element_type=F32)
            with_im = lax.dot_general(pair, weight_ref[slot, 1], NT, preferred_element_type=F32)
            out_re = with_re[:32] - with_im[32:]
            out_im = with_re[32:] + with_im[:32]
            for part, out in enumerate((out_re, out_im)):
                for half in range(2):
                    for p in range(2):
                        at = half * 16 + p * 8
                        lanes = slice(p * 256, p * 256 + 256)
                        beam_out_ref[0, slot, part, half * 8 : half * 8 + 8, lanes] = out[at : at + 8]

    cols = pl.ds(pl.multiple_of(pl.program_id(0) * 256, 256), 256)
    scale = 1.0 / 512
    for part, left in enumerate((plain_ref, turned_ref)):
        total = lax.dot_general(left[...], plain_ref[cols, :], NT, preferred_element_type=F32)
        vis_ref[part, 0, 0] = total * scale


def correlate(plain, turned, beam, weight, station_index):
    once = pl.Buffered(1)

    def whole(x):
        zeros = (0,) * len(x.shape)
        return pl.BlockSpec(x.shape, lambda i: zeros, pipeline_mode=once)

    beam_out = jax.ShapeDtypeStruct((1, PER_DEV, 2, FRAMES, 512), F32)
    operands = (plain, turned, beam, weight, station_index)
    return pl.pallas_call(
        correlate_kernel,
        grid=(4,),
        out_shape=[jax.ShapeDtypeStruct((2, 1, 1, SIGNALS, SIGNALS), F32), beam_out],
        in_specs=[whole(x) for x in operands],
        out_specs=[
            pl.BlockSpec((2, 1, 1, SIGNALS, 256), lambda i: (0, 0, 0, 0, i)),
            whole(beam_out),
        ],
        scratch_shapes=[pltpu.VMEM((2048, 128), F32)],
        compiler_params=pltpu.CompilerParams(vmem_limit_bytes=VMEM_LIMIT),
        name="correlate",
    )(*operands)


def body(volts, prototype, beam_channels, station_index, delays, gains, assign):
    sb_here = lax.axis_index("sb")
    st_here = lax.axis_index("st")
    owners = assign[:, 0]
    order = jnp.arange(owners.shape[0], dtype=jnp.int32)
    matches = (owners == sb_here).astype(jnp.int32)
    position = jnp.sum((order[None, :] < order[:, None]).astype(jnp.int32) * matches[None, :], axis=1)
    row = jnp.arange(256, dtype=jnp.int32)
    slot = jnp.where((row & 7) < PER_DEV, (row >> 3) * PER_DEV + (row & 7), -1)
    picker = matches[None, :] * (position[None, :] == slot[:, None]).astype(jnp.int32)
    filled = jnp.sum(picker, axis=1)
    slot_channel = jnp.sum(picker * beam_channels[None, :], axis=1)
    line = jnp.arange(1024, dtype=jnp.int32)
    main = sb_here * BAND + (line & 255) * 4 + (line >> 8)
    mine = lax.dynamic_slice_in_dim(slot_channel, st_here * 8, 8)[None]
    there = lax.dynamic_slice_in_dim(filled, st_here * 8, 8)[None]
    chan = jnp.concatenate([main, slot_channel])[:, None]
    plain, turned, beam, weight = exchange(volts, prototype, chan, delays, gains, mine, there)
    rows = (SIGNALS, 1024)
    return tuple(correlate(plain.reshape(rows), turned.reshape(rows), beam, weight, station_index[None]))


def solution(mesh):
    in_specs = (P(None, "st", None), P(), P(), P(), P(), P(), P())
    out_specs = (P(None, "sb", "st", None, None), P("sb", "st", None, None, None))
    return jax.shard_map(body, mesh=mesh, in_specs=in_specs, out_specs=out_specs, check_vma=False)
```

```python
import math

import jax
import jax.numpy as jnp
from jax import lax
from jax.experimental import pallas as pl
from jax.experimental.pallas import tpu as pltpu
from jax.sharding import PartitionSpec as P

NCH = 4096
FRAMES = 16
TAPS = 16
SLOTS = 160
BAND = 1024
GROUPS = 32
PER_DEV = 5
QUARTER = 1024
SIG = 16
SIGNALS = 1024
ROWS = 80
NT = (((1,), (1,)), ((), ()))
F32 = jnp.float32
BF16 = jnp.bfloat16
VMEM_LIMIT = 56 << 20
MESH = pl.DeviceIdType.MESH
PIECES = ((0, 48), (48, 32))
HALF = 8
CHIPS = ((2, 2), (1, 2), (2, 1), (3, 2), (2, 3), (0, 2), (2, 0), (1, 1), (3, 3), (1, 3), (3, 1), (0, 1), (3, 0), (0, 3), (1, 0))
ORDER = tuple((z, x, c) for z, x in CHIPS for c in range(2)) + ((0, 0, 1),)


def sincos_turns(turns):
    quarter = jnp.floor(turns * 4.0 + 0.5)
    x = (turns - quarter * 0.25) * (2.0 * math.pi)
    z = x * x
    sin_x = x * (1.0 + z * (-1.0 / 6 + z * (1.0 / 120 + z * (-1.0 / 5040 + z * (1.0 / 362880)))))
    cos_x = 1.0 + z * (-0.5 + z * (1.0 / 24 + z * (-1.0 / 720 + z * (1.0 / 40320))))
    which = quarter.astype(jnp.int32) & 3
    odd = (which & 1) == 1
    s = jnp.where(odd, cos_x, sin_x)
    c = jnp.where(odd, sin_x, cos_x)
    s = jnp.where(which >= 2, -s, s)
    c = jnp.where((which == 1) | (which == 2), -c, c)
    return s, c


def fill_slots(owner_ref, channel_ref, slots):
    entries = owner_ref.shape[1]
    match = owner_ref[...] == lax.axis_index("sb")
    ones = jnp.broadcast_to(match.astype(F32), (8, entries)).astype(BF16)
    row = lax.broadcasted_iota(jnp.int32, (entries, entries), 0)
    col = lax.broadcasted_iota(jnp.int32, (entries, entries), 1)
    earlier = (row < col).astype(F32).astype(BF16)
    position = jnp.dot(ones, earlier, preferred_element_type=F32)[0:1].astype(jnp.int32)
    position = jnp.where(match, position, -1)
    line = lax.broadcasted_iota(jnp.int32, (SLOTS, entries), 0)
    pick = (position == (line & 31) * PER_DEV + (line >> 5)).astype(F32)
    chan = jnp.sum(pick * channel_ref[...].astype(F32), axis=1, keepdims=True)
    filled = jnp.sum(pick, axis=1, keepdims=True)
    slots[0] = jnp.broadcast_to(chan, (SLOTS, 256))
    slots[1] = jnp.broadcast_to(filled, (SLOTS, 256))


def fill_tables(slots, table):
    def fill(wide, which, cos_row, sin_row):
        lane = lax.broadcasted_iota(jnp.int32, (32, 128), 1)
        s, c = sincos_turns(((lane * wide) & (NCH - 1)).astype(F32) * (1.0 / NCH))
        s_step, c_step = sincos_turns(((128 * wide) & (NCH - 1)).astype(F32) * (1.0 / NCH))
        s, c = s * (1.0 / 64), c * (1.0 / 64)
        cos_at = pl.ds(pl.multiple_of(cos_row, 32), 32)
        sin_at = pl.ds(pl.multiple_of(sin_row, 32), 32)
        for tile in range(QUARTER // 128):
            lanes = slice(tile * 128, tile * 128 + 128)
            table[which, cos_at, lanes] = c.astype(BF16)
            table[which, sin_at, lanes] = s.astype(BF16)
            s, c = s * c_step + c * s_step, c * c_step - s * s_step

    first = lax.axis_index("sb") * BAND

    @pl.loop(0, 32)
    def _(block):
        k1, row = block // 8, (block % 8) * 32
        line = lax.broadcasted_iota(jnp.int32, (32, 128), 0)
        fill(first + (row + line) * 4 + k1, k1, row, row + 256)

    @pl.loop(0, SLOTS // 32)
    def _(block):
        rows = pl.ds(pl.multiple_of(block * 32, 32), 32)
        fill(slots[0, rows, 0:128].astype(jnp.int32), 4, block * 32, block * 32 + SLOTS)


def filter_frames(volts, half, proto_ref, filt, spec):
    @pl.loop(0, QUARTER // 128)
    def _(tile):
        @pl.loop(0, 4)
        def _(n1):
            base = pl.multiple_of(n1 * QUARTER + tile * 128, 128)
            taps = [
                jnp.broadcast_to(proto_ref[t : t + 1, pl.ds(base, 128)], (SIG, 128))
                for t in range(TAPS)
            ]
            h0, h1 = taps[0::2], taps[1::2]
            hd = [b - a for a, b in zip(h0, h1)]
            for part in range(2):

                def frame(u):
                    at = pl.multiple_of((half * HALF + u) * NCH + base, 128)
                    return volts[part, :, pl.ds(at, 128)].astype(F32)

                acc = [[None] * (HALF // 2) for _ in range(3)]
                x0 = frame(0)
                for j in range((HALF + TAPS) // 2 - 1):
                    x1, after = frame(2 * j + 1), frame(2 * j + 2)
                    terms = ((hd, x1), (h0, x0 + x1), (h1, x1 + after))
                    for m in range(HALF // 2):
                        i = j - m
                        if 0 <= i < TAPS // 2:
                            for total, (h, x) in zip(acc, terms):
                                total[m] = h[i] * x if total[m] is None else total[m] + h[i] * x
                    x0 = after
                for m in range(HALF // 2):
                    filt[part * 4 + n1, 2 * m] = acc[1][m] + acc[0][m]
                    filt[part * 4 + n1, 2 * m + 1] = acc[2][m] - acc[0][m]

        lanes = pl.ds(pl.multiple_of(tile * 128, 128), 128)
        for f in range(HALF):
            re = [filt[n1, f] for n1 in range(4)]
            im = [filt[4 + n1, f] for n1 in range(4)]
            ar, ai = re[0] + re[2], im[0] + im[2]
            br, bi = re[0] - re[2], im[0] - im[2]
            cr, ci = re[1] + re[3], im[1] + im[3]
            dr, di = re[1] - re[3], im[1] - im[3]
            outs = [(ar + cr, ai + ci), (br + di, bi - dr), (ar - cr, ai - ci), (br - di, bi + dr)]
            for k1 in range(4):
                for part in range(2):
                    at = part * 128 + f * SIG
                    spec[k1, at : at + SIG, lanes] = outs[k1][part].astype(BF16)


def by_group(re, im):
    joined = jnp.concatenate([re.reshape(32, 8, 128), im.reshape(32, 8, 128)], axis=1)
    return joined.astype(BF16)


def exchange_kernel(
    volts_hbm, proto_ref, owner_ref, channel_ref, delay_ref, gain_ref,
    plain_hbm, turned_hbm, beam_hbm, weight_hbm,
    volts, slots, place, table, filt, spec, send, recv, plain, turned, weight,
    load_sem, own_sem, send_sem, recv_sem, out_sem,
):
    n = GROUPS
    me = lax.axis_index("st")

    def load(g):
        src = volts_hbm.at[:, pl.ds(g * SIG, SIG), :]
        return pltpu.make_async_copy(src, volts.at[g], load_sem.at[g])

    load(0).start()
    barrier = pltpu.get_barrier_semaphore()

    @pl.loop(1, n)
    def _(d):
        there = lax.rem(me + d, n)
        pl.semaphore_signal(barrier, inc=1, device_id={"st": there}, device_id_type=MESH)

    fill_slots(owner_ref, channel_ref, slots)
    fill_tables(slots, table)
    row = lax.broadcasted_iota(jnp.int32, (512, 2 * SLOTS), 0)
    col = lax.broadcasted_iota(jnp.int32, (512, 2 * SLOTS), 1)
    taken = ((row >> 3) & 1) * SLOTS + (row & 7) * 32 + (row >> 4)
    place[...] = ((taken == col) & ((row & 7) < PER_DEV)).astype(F32).astype(BF16)
    load(1).start()
    pl.semaphore_wait(barrier, n - 1)

    def own(q):
        return pltpu.make_async_copy(send.at[q, me], recv.at[q, me], own_sem.at[q])

    def remote(q, piece, there):
        rows = pl.ds(*PIECES[piece])
        return pltpu.make_async_remote_copy(
            src_ref=send.at[q, there, rows],
            dst_ref=recv.at[q, me, rows],
            send_sem=send_sem.at[q, piece],
            recv_sem=recv_sem.at[q, piece],
            device_id={"st": there},
            device_id_type=MESH,
        )

    def start(q, piece):
        plane, column, core = me // 8, (me // 2) % 4, me % 2
        for dz, dx, dc in ORDER:
            there = ((plane + dz) % 4) * 8 + ((column + dx) % 4) * 2 + (core + dc) % 2
            remote(q, piece, there).start()

    @pl.loop(0, 4)
    def _(step):
        g, half = step // 2, step % 2
        q = half * 2 + g

        @pl.when(half == 0)
        def _():
            src = volts_hbm.at[:, pl.ds(g * SIG, SIG), :]
            pltpu.make_async_copy(src, volts.at[g], load_sem.at[g]).wait()

        filter_frames(volts.at[g], half, proto_ref, filt, spec)

        def both(k1, which, rows):
            t = lax.dot_general(table[which, : 2 * rows], spec[k1], NT, preferred_element_type=F32)
            c, s = t[:rows], t[rows:]
            return c[:, :128] + s[:, 128:], c[:, 128:] - s[:, :128]

        chan = slots[0, :, 0:128].astype(jnp.int32)
        beam_re = jnp.zeros((SLOTS, 128), F32)
        beam_im = jnp.zeros((SLOTS, 128), F32)
        for k1 in range(4):
            re, im = both(k1, 4, SLOTS)
            mine = (chan & 3) == k1
            beam_re = jnp.where(mine, re, beam_re)
            beam_im = jnp.where(mine, im, beam_im)
        row = lax.broadcasted_iota(jnp.int32, (128, 128), 0)
        col = lax.broadcasted_iota(jnp.int32, (128, 128), 1)
        turn = (row == (col & 7) * 16 + (col >> 3)).astype(F32).astype(BF16)
        joined = jnp.concatenate([beam_re, beam_im], axis=0).astype(BF16)
        joined = jnp.dot(joined, turn, preferred_element_type=F32).astype(BF16)
        placed = jnp.dot(place[...], joined, preferred_element_type=F32)
        send[q, :, 0:16, :] = placed.astype(BF16).reshape(32, 16, 128)
        for k1 in range(4):
            re, im = both(k1, k1, 256)
            send[q, :, 16 + k1 * 16 : 32 + k1 * 16, :] = by_group(re, im)
            if k1 % 2 == 1:
                start(q, k1 // 2)
        own(q).start()

    @pl.loop(0, delay_ref.shape[0] // 32)
    def _(block):
        at = pl.ds(pl.multiple_of(block * 32, 32), 32)
        scaling = gain_ref[at, :] * (1.0 / math.sqrt(gain_ref.shape[1]))
        for slot in range(PER_DEV):
            mine = pl.ds(slot * 32 + me, 1)
            turns = delay_ref[at, :] * (slots[0, mine, :] * (1.0 / NCH))
            turns = turns - jnp.floor(turns)
            s, c = sincos_turns(turns)
            level = scaling * slots[1, mine, :]
            weight[slot, 0, at, :] = (level * c).astype(BF16)
            weight[slot, 1, at, :] = (-level * s).astype(BF16)

    copies = [pltpu.make_async_copy(weight, weight_hbm, out_sem.at[0])]
    copies[0].start()
    for g in range(2):
        for q in (g, 2 + g):
            own(q).wait()
            for piece in range(len(PIECES)):
                rows = pl.ds(*PIECES[piece])
                others = pl.ds(0, n - 1)
                all_of = pltpu.make_async_remote_copy(
                    src_ref=send.at[q, others, rows],
                    dst_ref=recv.at[q, others, rows],
                    send_sem=send_sem.at[q, piece],
                    recv_sem=recv_sem.at[q, piece],
                    device_id={"st": lax.rem(me + 1, n)},
                    device_id_type=MESH,
                )
                all_of.wait_send()
                all_of.wait_recv()
            beam = pltpu.make_async_copy(recv.at[q, :, 0:16], beam_hbm.at[q], out_sem.at[1 + q])
            beam.start()
            copies.append(beam)

        @pl.loop(0, n)
        def _(src):
            block = jnp.concatenate([recv[g, src, 16:80, :], recv[2 + g, src, 16:80, :]], axis=0)
            block = block.astype(F32)
            by_part = block.reshape(8, 2, 8, 128)
            swapped = jnp.stack([by_part[:, 1], -by_part[:, 0]], axis=1).reshape(128, 128)
            for x, dest in ((block, plain), (swapped, turned)):
                t = x.T.astype(BF16)
                for f in range(HALF):
                    dest[src, g, :, f * 128 : f * 128 + 128] = t[f * SIG : f * SIG + SIG]

        for i, (mem, out) in enumerate(((plain, plain_hbm), (turned, turned_hbm))):
            copy = pltpu.make_async_copy(mem.at[:, g], out.at[:, g], out_sem.at[5 + 2 * g + i])
            copy.start()
            copies.append(copy)
    for copy in copies:
        copy.wait()


def exchange(volts, prototype, owners, channels, delays, gains):
    vmem = pl.BlockSpec(memory_space=pltpu.VMEM)
    hbm = pl.BlockSpec(memory_space=pl.ANY)
    blocks = (4, GROUPS, ROWS, 128)
    spectra = (GROUPS, 2, SIG, 1024)
    weight = (PER_DEV, 2) + delays.shape
    return pl.pallas_call(
        exchange_kernel,
        out_shape=[
            jax.ShapeDtypeStruct(spectra, BF16),
            jax.ShapeDtypeStruct(spectra, BF16),
            jax.ShapeDtypeStruct((4, GROUPS, 16, 128), BF16),
            jax.ShapeDtypeStruct(weight, BF16),
        ],
        in_specs=[hbm] + [vmem] * 5,
        out_specs=[hbm] * 4,
        scratch_shapes=[
            pltpu.VMEM((2, 2, SIG, volts.shape[2]), BF16),
            pltpu.VMEM((2, SLOTS, 256), F32),
            pltpu.VMEM((512, 2 * SLOTS), BF16),
            pltpu.VMEM((5, 512, QUARTER), BF16),
            pltpu.VMEM((8, HALF, SIG, 128), F32),
            pltpu.VMEM((4, 256, QUARTER), BF16),
            pltpu.VMEM(blocks, BF16),
            pltpu.VMEM(blocks, BF16),
            pltpu.VMEM(spectra, BF16),
            pltpu.VMEM(spectra, BF16),
            pltpu.VMEM(weight, BF16),
            pltpu.SemaphoreType.DMA((2,)),
            pltpu.SemaphoreType.DMA((4,)),
            pltpu.SemaphoreType.DMA((4, len(PIECES))),
            pltpu.SemaphoreType.DMA((4, len(PIECES))),
            pltpu.SemaphoreType.DMA((9,)),
        ],
        compiler_params=pltpu.CompilerParams(
            vmem_limit_bytes=VMEM_LIMIT, collective_id=0, has_side_effects=True
        ),
        name="exchange",
    )(volts, prototype, owners, channels, delays, gains)


def correlate_kernel(plain_ref, turned_ref, beam_ref, weight_ref, station_ref, vis_ref, beam_out_ref, wide):
    @pl.when(pl.program_id(0) == 0)
    def _():
        listed = station_ref.shape[1]
        row = lax.broadcasted_iota(jnp.int32, (512, listed), 0)
        station = (row & 31) * 16 + ((row >> 5) & 1) * 8 + (row >> 6)
        select = (station == station_ref[...]).astype(F32).astype(BF16)
        wide[...] = beam_ref[...].reshape(4 * 512, 128).astype(F32)
        rows = []
        for slot in range(PER_DEV):
            for part in range(2):
                for half in range(2):
                    first = half * 1024 + part * 8 + slot
                    x = wide[pl.ds(first, 64, stride=16), :]
                    t = x.T.astype(BF16)
                    rows.append(jnp.concatenate([t[s * 16 : s * 16 + 16] for s in range(8)], axis=1))
        picked = jnp.dot(jnp.concatenate(rows, axis=0), select, preferred_element_type=F32).astype(BF16)
        for slot in range(PER_DEV):
            pair = picked[slot * 64 : slot * 64 + 64]
            with_re = lax.dot_general(pair, weight_ref[slot, 0], NT, preferred_element_type=F32)
            with_im = lax.dot_general(pair, weight_ref[slot, 1], NT, preferred_element_type=F32)
            out_re = with_re[:32] - with_im[32:]
            out_im = with_re[32:] + with_im[:32]
            for part, out in enumerate((out_re, out_im)):
                for half in range(2):
                    for p in range(2):
                        at = half * 16 + p * 8
                        lanes = slice(p * 256, p * 256 + 256)
                        beam_out_ref[0, slot, part, half * 8 : half * 8 + 8, lanes] = out[at : at + 8]

    cols = pl.ds(pl.multiple_of(pl.program_id(0) * 256, 256), 256)
    scale = 1.0 / 512
    for part, left in enumerate((plain_ref, turned_ref)):
        total = lax.dot_general(left[...], plain_ref[cols, :], NT, preferred_element_type=F32)
        vis_ref[part, 0, 0] = total * scale


def correlate(plain, turned, beam, weight, station_index):
    once = pl.Buffered(1)

    def whole(x):
        zeros = (0,) * len(x.shape)
        return pl.BlockSpec(x.shape, lambda i: zeros, pipeline_mode=once)

    beam_out = jax.ShapeDtypeStruct((1, PER_DEV, 2, FRAMES, 512), F32)
    operands = (plain, turned, beam, weight, station_index)
    return pl.pallas_call(
        correlate_kernel,
        grid=(4,),
        out_shape=[jax.ShapeDtypeStruct((2, 1, 1, SIGNALS, SIGNALS), F32), beam_out],
        in_specs=[whole(x) for x in operands],
        out_specs=[
            pl.BlockSpec((2, 1, 1, SIGNALS, 256), lambda i: (0, 0, 0, 0, i)),
            whole(beam_out),
        ],
        scratch_shapes=[pltpu.VMEM((2048, 128), F32)],
        compiler_params=pltpu.CompilerParams(vmem_limit_bytes=VMEM_LIMIT),
        name="correlate",
    )(*operands)


def body(volts, prototype, beam_channels, station_index, delays, gains, assign):
    owners = assign.reshape(1, -1)
    plain, turned, beam, weight = exchange(volts, prototype, owners, beam_channels[None], delays, gains)
    rows = (SIGNALS, 1024)
    return tuple(correlate(plain.reshape(rows), turned.reshape(rows), beam, weight, station_index[None]))


def solution(mesh):
    in_specs = (P(None, "st", None), P(), P(), P(), P(), P(), P())
    out_specs = (P(None, "sb", "st", None, None), P("sb", "st", None, None, None))
    return jax.shard_map(body, mesh=mesh, in_specs=in_specs, out_specs=out_specs, check_vma=False)
```

```python
import math

import jax
import jax.numpy as jnp
from jax import lax
from jax.experimental import pallas as pl
from jax.experimental.pallas import tpu as pltpu
from jax.sharding import PartitionSpec as P

NCH = 4096
FRAMES = 16
TAPS = 16
SLOTS = 160
BAND = 1024
GROUPS = 32
PER_DEV = 5
QUARTER = 1024
SIG = 16
SIGNALS = 1024
ROWS = 80
NT = (((1,), (1,)), ((), ()))
F32 = jnp.float32
BF16 = jnp.bfloat16
VMEM_LIMIT = 56 << 20
MESH = pl.DeviceIdType.MESH
PIECES = ((0, 48), (48, 32))
HALF = 8
CHIPS = ((2, 2), (1, 2), (2, 1), (3, 2), (2, 3), (0, 2), (2, 0), (1, 1), (3, 3), (1, 3), (3, 1), (0, 1), (3, 0), (0, 3), (1, 0))
ORDER = tuple((z, x, c) for z, x in CHIPS for c in range(2)) + ((0, 0, 1),)


def sincos_turns(turns):
    quarter = jnp.floor(turns * 4.0 + 0.5)
    x = (turns - quarter * 0.25) * (2.0 * math.pi)
    z = x * x
    sin_x = x * (1.0 + z * (-1.0 / 6 + z * (1.0 / 120 + z * (-1.0 / 5040 + z * (1.0 / 362880)))))
    cos_x = 1.0 + z * (-0.5 + z * (1.0 / 24 + z * (-1.0 / 720 + z * (1.0 / 40320))))
    which = quarter.astype(jnp.int32) & 3
    odd = (which & 1) == 1
    s = jnp.where(odd, cos_x, sin_x)
    c = jnp.where(odd, sin_x, cos_x)
    s = jnp.where(which >= 2, -s, s)
    c = jnp.where((which == 1) | (which == 2), -c, c)
    return s, c


def fill_slots(owner_ref, channel_ref, slots):
    entries = owner_ref.shape[1]
    match = owner_ref[...] == lax.axis_index("sb")
    ones = jnp.broadcast_to(match.astype(F32), (8, entries)).astype(BF16)
    row = lax.broadcasted_iota(jnp.int32, (entries, entries), 0)
    col = lax.broadcasted_iota(jnp.int32, (entries, entries), 1)
    earlier = (row < col).astype(F32).astype(BF16)
    position = jnp.dot(ones, earlier, preferred_element_type=F32)[0:1].astype(jnp.int32)
    position = jnp.where(match, position, -1)
    line = lax.broadcasted_iota(jnp.int32, (SLOTS, entries), 0)
    pick = (position == (line & 31) * PER_DEV + (line >> 5)).astype(F32)
    chan = jnp.sum(pick * channel_ref[...].reshape(1, entries).astype(F32), axis=1, keepdims=True)
    filled = jnp.sum(pick, axis=1, keepdims=True)
    slots[0] = jnp.broadcast_to(chan, (SLOTS, 256))
    slots[1] = jnp.broadcast_to(filled, (SLOTS, 256))


def fill_tables(slots, table):
    def fill(wide, which, cos_row, sin_row):
        lane = lax.broadcasted_iota(jnp.int32, (32, 128), 1)
        s, c = sincos_turns(((lane * wide) & (NCH - 1)).astype(F32) * (1.0 / NCH))
        s_step, c_step = sincos_turns(((128 * wide) & (NCH - 1)).astype(F32) * (1.0 / NCH))
        s, c = s * (1.0 / 64), c * (1.0 / 64)
        cos_at = pl.ds(pl.multiple_of(cos_row, 32), 32)
        sin_at = pl.ds(pl.multiple_of(sin_row, 32), 32)
        for tile in range(QUARTER // 128):
            lanes = slice(tile * 128, tile * 128 + 128)
            table[which, cos_at, lanes] = c.astype(BF16)
            table[which, sin_at, lanes] = s.astype(BF16)
            s, c = s * c_step + c * s_step, c * c_step - s * s_step

    first = lax.axis_index("sb") * BAND

    @pl.loop(0, 32)
    def _(block):
        k1, row = block // 8, (block % 8) * 32
        line = lax.broadcasted_iota(jnp.int32, (32, 128), 0)
        fill(first + (row + line) * 4 + k1, k1, row, row + 256)

    @pl.loop(0, SLOTS // 32)
    def _(block):
        rows = pl.ds(pl.multiple_of(block * 32, 32), 32)
        fill(slots[0, rows, 0:128].astype(jnp.int32), 4, block * 32, block * 32 + SLOTS)


def filter_frames(volts, half, proto_ref, filt, spec):
    @pl.loop(0, QUARTER // 128)
    def _(tile):
        @pl.loop(0, 4)
        def _(n1):
            base = pl.multiple_of(n1 * QUARTER + tile * 128, 128)
            taps = [
                jnp.broadcast_to(proto_ref[t : t + 1, pl.ds(base, 128)], (SIG, 128))
                for t in range(TAPS)
            ]
            h0, h1 = taps[0::2], taps[1::2]
            hd = [b - a for a, b in zip(h0, h1)]
            for part in range(2):

                def frame(u):
                    at = pl.multiple_of((half * HALF + u) * NCH + base, 128)
                    return volts[part, :, pl.ds(at, 128)].astype(F32)

                acc = [[None] * (HALF // 2) for _ in range(3)]
                x0 = frame(0)
                for j in range((HALF + TAPS) // 2 - 1):
                    x1, after = frame(2 * j + 1), frame(2 * j + 2)
                    terms = ((hd, x1), (h0, x0 + x1), (h1, x1 + after))
                    for m in range(HALF // 2):
                        i = j - m
                        if 0 <= i < TAPS // 2:
                            for total, (h, x) in zip(acc, terms):
                                total[m] = h[i] * x if total[m] is None else total[m] + h[i] * x
                    x0 = after
                for m in range(HALF // 2):
                    filt[part * 4 + n1, 2 * m] = acc[1][m] + acc[0][m]
                    filt[part * 4 + n1, 2 * m + 1] = acc[2][m] - acc[0][m]

        lanes = pl.ds(pl.multiple_of(tile * 128, 128), 128)
        for f in range(HALF):
            re = [filt[n1, f] for n1 in range(4)]
            im = [filt[4 + n1, f] for n1 in range(4)]
            ar, ai = re[0] + re[2], im[0] + im[2]
            br, bi = re[0] - re[2], im[0] - im[2]
            cr, ci = re[1] + re[3], im[1] + im[3]
            dr, di = re[1] - re[3], im[1] - im[3]
            outs = [(ar + cr, ai + ci), (br + di, bi - dr), (ar - cr, ai - ci), (br - di, bi + dr)]
            for k1 in range(4):
                for part in range(2):
                    at = part * 128 + f * SIG
                    spec[k1, at : at + SIG, lanes] = outs[k1][part].astype(BF16)


def by_group(re, im):
    joined = jnp.concatenate([re.reshape(32, 8, 128), im.reshape(32, 8, 128)], axis=1)
    return joined.astype(BF16)


def exchange_kernel(
    volts_hbm, proto_ref, owner_ref, channel_ref, delay_ref, gain_ref,
    plain_hbm, turned_hbm, beam_hbm, weight_hbm,
    volts, slots, place, table, filt, spec, send, recv, plain, turned, weight,
    load_sem, own_sem, send_sem, recv_sem, out_sem,
):
    n = GROUPS
    me = lax.axis_index("st")

    def load(g):
        src = volts_hbm.at[:, pl.ds(g * SIG, SIG), :]
        return pltpu.make_async_copy(src, volts.at[g], load_sem.at[g])

    load(0).start()
    barrier = pltpu.get_barrier_semaphore()

    @pl.loop(1, n)
    def _(d):
        there = lax.rem(me + d, n)
        pl.semaphore_signal(barrier, inc=1, device_id={"st": there}, device_id_type=MESH)

    fill_slots(owner_ref, channel_ref, slots)
    fill_tables(slots, table)
    row = lax.broadcasted_iota(jnp.int32, (512, 2 * SLOTS), 0)
    col = lax.broadcasted_iota(jnp.int32, (512, 2 * SLOTS), 1)
    taken = ((row >> 3) & 1) * SLOTS + (row & 7) * 32 + (row >> 4)
    place[...] = ((taken == col) & ((row & 7) < PER_DEV)).astype(F32).astype(BF16)
    load(1).start()
    pl.semaphore_wait(barrier, n - 1)

    def own(q):
        return pltpu.make_async_copy(send.at[q, me], recv.at[q, me], own_sem.at[q])

    def remote(q, piece, there):
        rows = pl.ds(*PIECES[piece])
        return pltpu.make_async_remote_copy(
            src_ref=send.at[q, there, rows],
            dst_ref=recv.at[q, me, rows],
            send_sem=send_sem.at[q, piece],
            recv_sem=recv_sem.at[q, piece],
            device_id={"st": there},
            device_id_type=MESH,
        )

    def start(q, piece):
        plane, column, core = me // 8, (me // 2) % 4, me % 2
        for dz, dx, dc in ORDER:
            there = ((plane + dz) % 4) * 8 + ((column + dx) % 4) * 2 + (core + dc) % 2
            remote(q, piece, there).start()

    @pl.loop(0, 4)
    def _(step):
        g, half = step // 2, step % 2
        q = half * 2 + g

        @pl.when(half == 0)
        def _():
            src = volts_hbm.at[:, pl.ds(g * SIG, SIG), :]
            pltpu.make_async_copy(src, volts.at[g], load_sem.at[g]).wait()

        filter_frames(volts.at[g], half, proto_ref, filt, spec)

        def both(k1, which, rows):
            t = lax.dot_general(table[which, : 2 * rows], spec[k1], NT, preferred_element_type=F32)
            c, s = t[:rows], t[rows:]
            return c[:, :128] + s[:, 128:], c[:, 128:] - s[:, :128]

        chan = slots[0, :, 0:128].astype(jnp.int32)
        beam_re = jnp.zeros((SLOTS, 128), F32)
        beam_im = jnp.zeros((SLOTS, 128), F32)
        for k1 in range(4):
            re, im = both(k1, 4, SLOTS)
            mine = (chan & 3) == k1
            beam_re = jnp.where(mine, re, beam_re)
            beam_im = jnp.where(mine, im, beam_im)
        row = lax.broadcasted_iota(jnp.int32, (128, 128), 0)
        col = lax.broadcasted_iota(jnp.int32, (128, 128), 1)
        turn = (row == (col & 7) * 16 + (col >> 3)).astype(F32).astype(BF16)
        joined = jnp.concatenate([beam_re, beam_im], axis=0).astype(BF16)
        joined = jnp.dot(joined, turn, preferred_element_type=F32).astype(BF16)
        placed = jnp.dot(place[...], joined, preferred_element_type=F32)
        send[q, :, 0:16, :] = placed.astype(BF16).reshape(32, 16, 128)
        for k1 in range(4):
            re, im = both(k1, k1, 256)
            send[q, :, 16 + k1 * 16 : 32 + k1 * 16, :] = by_group(re, im)
            if k1 % 2 == 1:
                start(q, k1 // 2)
        own(q).start()

    @pl.loop(0, delay_ref.shape[0] // 32)
    def _(block):
        at = pl.ds(pl.multiple_of(block * 32, 32), 32)
        scaling = gain_ref[at, :] * (1.0 / math.sqrt(gain_ref.shape[1]))
        for slot in range(PER_DEV):
            mine = pl.ds(slot * 32 + me, 1)
            turns = delay_ref[at, :] * (slots[0, mine, :] * (1.0 / NCH))
            turns = turns - jnp.floor(turns)
            s, c = sincos_turns(turns)
            level = scaling * slots[1, mine, :]
            weight[slot, 0, at, :] = (level * c).astype(BF16)
            weight[slot, 1, at, :] = (-level * s).astype(BF16)

    copies = [pltpu.make_async_copy(weight, weight_hbm, out_sem.at[0])]
    copies[0].start()
    for g in range(2):
        for q in (g, 2 + g):
            own(q).wait()
            for piece in range(len(PIECES)):
                rows = pl.ds(*PIECES[piece])
                others = pl.ds(0, n - 1)
                all_of = pltpu.make_async_remote_copy(
                    src_ref=send.at[q, others, rows],
                    dst_ref=recv.at[q, others, rows],
                    send_sem=send_sem.at[q, piece],
                    recv_sem=recv_sem.at[q, piece],
                    device_id={"st": lax.rem(me + 1, n)},
                    device_id_type=MESH,
                )
                all_of.wait_send()
                all_of.wait_recv()
            beam = pltpu.make_async_copy(recv.at[q, :, 0:16], beam_hbm.at[q], out_sem.at[1 + q])
            beam.start()
            copies.append(beam)

        @pl.loop(0, n)
        def _(src):
            block = jnp.concatenate([recv[g, src, 16:80, :], recv[2 + g, src, 16:80, :]], axis=0)
            block = block.astype(F32)
            by_part = block.reshape(8, 2, 8, 128)
            swapped = jnp.stack([by_part[:, 1], -by_part[:, 0]], axis=1).reshape(128, 128)
            for x, dest in ((block, plain), (swapped, turned)):
                t = x.astype(BF16).T
                for f in range(HALF):
                    dest[src, g, :, f * 128 : f * 128 + 128] = t[f * SIG : f * SIG + SIG]

        for i, (mem, out) in enumerate(((plain, plain_hbm), (turned, turned_hbm))):
            copy = pltpu.make_async_copy(mem.at[:, g], out.at[:, g], out_sem.at[5 + 2 * g + i])
            copy.start()
            copies.append(copy)
    for copy in copies:
        copy.wait()


def exchange(volts, prototype, owners, channels, delays, gains):
    vmem = pl.BlockSpec(memory_space=pltpu.VMEM)
    hbm = pl.BlockSpec(memory_space=pl.ANY)
    blocks = (4, GROUPS, ROWS, 128)
    spectra = (GROUPS, 2, SIG, 1024)
    weight = (PER_DEV, 2) + delays.shape
    return pl.pallas_call(
        exchange_kernel,
        out_shape=[
            jax.ShapeDtypeStruct(spectra, BF16),
            jax.ShapeDtypeStruct(spectra, BF16),
            jax.ShapeDtypeStruct((4, GROUPS, 16, 128), BF16),
            jax.ShapeDtypeStruct(weight, BF16),
        ],
        in_specs=[hbm] + [vmem] * 5,
        out_specs=[hbm] * 4,
        scratch_shapes=[
            pltpu.VMEM((2, 2, SIG, volts.shape[2]), BF16),
            pltpu.VMEM((2, SLOTS, 256), F32),
            pltpu.VMEM((512, 2 * SLOTS), BF16),
            pltpu.VMEM((5, 512, QUARTER), BF16),
            pltpu.VMEM((8, HALF, SIG, 128), F32),
            pltpu.VMEM((4, 256, QUARTER), BF16),
            pltpu.VMEM(blocks, BF16),
            pltpu.VMEM(blocks, BF16),
            pltpu.VMEM(spectra, BF16),
            pltpu.VMEM(spectra, BF16),
            pltpu.VMEM(weight, BF16),
            pltpu.SemaphoreType.DMA((2,)),
            pltpu.SemaphoreType.DMA((4,)),
            pltpu.SemaphoreType.DMA((4, len(PIECES))),
            pltpu.SemaphoreType.DMA((4, len(PIECES))),
            pltpu.SemaphoreType.DMA((9,)),
        ],
        compiler_params=pltpu.CompilerParams(
            vmem_limit_bytes=VMEM_LIMIT, collective_id=0, has_side_effects=True
        ),
        name="exchange",
    )(volts, prototype, owners, channels, delays, gains)


def correlate_kernel(plain_ref, turned_ref, beam_ref, weight_ref, station_ref, vis_ref, beam_out_ref, wide):
    @pl.when(pl.program_id(0) == 0)
    def _():
        listed = station_ref.shape[1]
        row = lax.broadcasted_iota(jnp.int32, (512, listed), 0)
        station = (row & 31) * 16 + ((row >> 5) & 1) * 8 + (row >> 6)
        select = (station == station_ref[...]).astype(F32).astype(BF16)
        wide[...] = beam_ref[...].reshape(4 * 512, 128).astype(F32)
        rows = []
        for slot in range(PER_DEV):
            for part in range(2):
                for half in range(2):
                    first = half * 1024 + part * 8 + slot
                    x = wide[pl.ds(first, 64, stride=16), :]
                    t = x.T.astype(BF16)
                    rows.append(jnp.concatenate([t[s * 16 : s * 16 + 16] for s in range(8)], axis=1))
        picked = jnp.dot(jnp.concatenate(rows, axis=0), select, preferred_element_type=F32).astype(BF16)
        for slot in range(PER_DEV):
            pair = picked[slot * 64 : slot * 64 + 64]
            with_re = lax.dot_general(pair, weight_ref[slot, 0], NT, preferred_element_type=F32)
            with_im = lax.dot_general(pair, weight_ref[slot, 1], NT, preferred_element_type=F32)
            out_re = with_re[:32] - with_im[32:]
            out_im = with_re[32:] + with_im[:32]
            for part, out in enumerate((out_re, out_im)):
                for half in range(2):
                    for p in range(2):
                        at = half * 16 + p * 8
                        lanes = slice(p * 256, p * 256 + 256)
                        beam_out_ref[0, slot, part, half * 8 : half * 8 + 8, lanes] = out[at : at + 8]

    cols = pl.ds(pl.multiple_of(pl.program_id(0) * 256, 256), 256)
    scale = 1.0 / 512
    for part, left in enumerate((plain_ref, turned_ref)):
        total = lax.dot_general(left[...], plain_ref[cols, :], NT, preferred_element_type=F32)
        vis_ref[part, 0, 0] = total * scale


def correlate(plain, turned, beam, weight, station_index):
    once = pl.Buffered(1)

    def whole(x):
        zeros = (0,) * len(x.shape)
        return pl.BlockSpec(x.shape, lambda i: zeros, pipeline_mode=once)

    beam_out = jax.ShapeDtypeStruct((1, PER_DEV, 2, FRAMES, 512), F32)
    operands = (plain, turned, beam, weight, station_index)
    return pl.pallas_call(
        correlate_kernel,
        grid=(4,),
        out_shape=[jax.ShapeDtypeStruct((2, 1, 1, SIGNALS, SIGNALS), F32), beam_out],
        in_specs=[whole(x) for x in operands],
        out_specs=[
            pl.BlockSpec((2, 1, 1, SIGNALS, 256), lambda i: (0, 0, 0, 0, i)),
            whole(beam_out),
        ],
        scratch_shapes=[pltpu.VMEM((2048, 128), F32)],
        compiler_params=pltpu.CompilerParams(vmem_limit_bytes=VMEM_LIMIT),
        name="correlate",
    )(*operands)


def body(volts, prototype, beam_channels, station_index, delays, gains, assign):
    owners = assign.reshape(1, -1)
    plain, turned, beam, weight = exchange(volts, prototype, owners, beam_channels, delays, gains)
    rows = (SIGNALS, 1024)
    return tuple(correlate(plain.reshape(rows), turned.reshape(rows), beam, weight, station_index[None]))


def solution(mesh):
    in_specs = (P(None, "st", None), P(), P(), P(), P(), P(), P())
    out_specs = (P(None, "sb", "st", None, None), P("sb", "st", None, None, None))
    return jax.shard_map(body, mesh=mesh, in_specs=in_specs, out_specs=out_specs, check_vma=False)
```

```python
import math

import jax
import jax.numpy as jnp
from jax import lax
from jax.experimental import pallas as pl
from jax.experimental.pallas import tpu as pltpu
from jax.sharding import PartitionSpec as P

NCH = 4096
FRAMES = 16
TAPS = 16
SLOTS = 160
BAND = 1024
GROUPS = 32
PER_DEV = 5
QUARTER = 1024
SIG = 16
SIGNALS = 1024
ROWS = 80
NT = (((1,), (1,)), ((), ()))
F32 = jnp.float32
BF16 = jnp.bfloat16
VMEM_LIMIT = 56 << 20
MESH = pl.DeviceIdType.MESH
PIECES = ((0, 48), (48, 32))
HALF = 8
CHIPS = ((2, 2), (1, 2), (2, 1), (3, 2), (2, 3), (0, 2), (2, 0), (1, 1), (3, 3), (1, 3), (3, 1), (0, 1), (3, 0), (0, 3), (1, 0))
ORDER = tuple((z, x, c) for z, x in CHIPS for c in range(2)) + ((0, 0, 1),)


def sincos_turns(turns):
    quarter = jnp.floor(turns * 4.0 + 0.5)
    x = (turns - quarter * 0.25) * (2.0 * math.pi)
    z = x * x
    sin_x = x * (1.0 + z * (-1.0 / 6 + z * (1.0 / 120 + z * (-1.0 / 5040 + z * (1.0 / 362880)))))
    cos_x = 1.0 + z * (-0.5 + z * (1.0 / 24 + z * (-1.0 / 720 + z * (1.0 / 40320))))
    which = quarter.astype(jnp.int32) & 3
    odd = (which & 1) == 1
    s = jnp.where(odd, cos_x, sin_x)
    c = jnp.where(odd, sin_x, cos_x)
    s = jnp.where(which >= 2, -s, s)
    c = jnp.where((which == 1) | (which == 2), -c, c)
    return s, c


def fill_slots(owner_ref, channel_ref, slots):
    entries = owner_ref.shape[1]
    match = owner_ref[...] == lax.axis_index("sb")
    ones = jnp.broadcast_to(match.astype(F32), (8, entries)).astype(BF16)
    row = lax.broadcasted_iota(jnp.int32, (entries, entries), 0)
    col = lax.broadcasted_iota(jnp.int32, (entries, entries), 1)
    earlier = (row < col).astype(F32).astype(BF16)
    position = jnp.dot(ones, earlier, preferred_element_type=F32)[0:1].astype(jnp.int32)
    position = jnp.where(match, position, -1)
    line = lax.broadcasted_iota(jnp.int32, (SLOTS, entries), 0)
    pick = (position == (line & 31) * PER_DEV + (line >> 5)).astype(F32)
    chan = jnp.sum(pick * channel_ref[...].reshape(1, entries).astype(F32), axis=1, keepdims=True)
    filled = jnp.sum(pick, axis=1, keepdims=True)
    slots[0] = jnp.broadcast_to(chan, (SLOTS, 256))
    slots[1] = jnp.broadcast_to(filled, (SLOTS, 256))


def fill_tables(slots, table):
    def fill(wide, which, cos_row, sin_row):
        lane = lax.broadcasted_iota(jnp.int32, (32, 128), 1)
        s, c = sincos_turns(((lane * wide) & (NCH - 1)).astype(F32) * (1.0 / NCH))
        s_step, c_step = sincos_turns(((128 * wide) & (NCH - 1)).astype(F32) * (1.0 / NCH))
        s, c = s * (1.0 / 64), c * (1.0 / 64)
        cos_at = pl.ds(pl.multiple_of(cos_row, 32), 32)
        sin_at = pl.ds(pl.multiple_of(sin_row, 32), 32)
        for tile in range(QUARTER // 128):
            lanes = slice(tile * 128, tile * 128 + 128)
            table[which, cos_at, lanes] = c.astype(BF16)
            table[which, sin_at, lanes] = s.astype(BF16)
            s, c = s * c_step + c * s_step, c * c_step - s * s_step

    first = lax.axis_index("sb") * BAND

    @pl.loop(0, 32)
    def _(block):
        k1, row = block // 8, (block % 8) * 32
        line = lax.broadcasted_iota(jnp.int32, (32, 128), 0)
        fill(first + (row + line) * 4 + k1, k1, row, row + 256)

    @pl.loop(0, SLOTS // 32)
    def _(block):
        rows = pl.ds(pl.multiple_of(block * 32, 32), 32)
        fill(slots[0, rows, 0:128].astype(jnp.int32), 4, block * 32, block * 32 + SLOTS)


def filter_frames(volts, half, proto_ref, filt, spec):
    @pl.loop(0, QUARTER // 128)
    def _(tile):
        @pl.loop(0, 4)
        def _(n1):
            base = pl.multiple_of(n1 * QUARTER + tile * 128, 128)
            taps = [
                jnp.broadcast_to(proto_ref[t : t + 1, pl.ds(base, 128)], (8, 128))
                for t in range(TAPS)
            ]
            h0, h1 = taps[0::2], taps[1::2]
            hd = [b - a for a, b in zip(h0, h1)]
            for part in range(2):
                for rows in (slice(0, 8), slice(8, 16)):

                    def frame(u):
                        at = pl.multiple_of((half * HALF + u) * NCH + base, 128)
                        return volts[part, rows, pl.ds(at, 128)].astype(F32)

                    acc = [[None] * (HALF // 2) for _ in range(3)]
                    x0 = frame(0)
                    for j in range((HALF + TAPS) // 2 - 1):
                        x1, after = frame(2 * j + 1), frame(2 * j + 2)
                        terms = ((hd, x1), (h0, x0 + x1), (h1, x1 + after))
                        for m in range(HALF // 2):
                            i = j - m
                            if 0 <= i < TAPS // 2:
                                for total, (h, x) in zip(acc, terms):
                                    total[m] = h[i] * x if total[m] is None else total[m] + h[i] * x
                        x0 = after
                    for m in range(HALF // 2):
                        filt[part * 4 + n1, 2 * m, rows] = acc[1][m] + acc[0][m]
                        filt[part * 4 + n1, 2 * m + 1, rows] = acc[2][m] - acc[0][m]

        lanes = pl.ds(pl.multiple_of(tile * 128, 128), 128)
        for f in range(HALF):
            re = [filt[n1, f] for n1 in range(4)]
            im = [filt[4 + n1, f] for n1 in range(4)]
            ar, ai = re[0] + re[2], im[0] + im[2]
            br, bi = re[0] - re[2], im[0] - im[2]
            cr, ci = re[1] + re[3], im[1] + im[3]
            dr, di = re[1] - re[3], im[1] - im[3]
            outs = [(ar + cr, ai + ci), (br + di, bi - dr), (ar - cr, ai - ci), (br - di, bi + dr)]
            for k1 in range(4):
                for part in range(2):
                    at = part * 128 + f * SIG
                    spec[k1, at : at + SIG, lanes] = outs[k1][part].astype(BF16)


def by_group(re, im):
    joined = jnp.concatenate([re.reshape(32, 8, 128), im.reshape(32, 8, 128)], axis=1)
    return joined.astype(BF16)


def exchange_kernel(
    volts_hbm, proto_ref, owner_ref, channel_ref, delay_ref, gain_ref,
    plain_hbm, turned_hbm, beam_hbm, weight_hbm,
    volts, slots, place, table, filt, spec, send, recv, plain, turned, weight,
    load_sem, own_sem, send_sem, recv_sem, out_sem,
):
    n = GROUPS
    me = lax.axis_index("st")

    def load(g):
        src = volts_hbm.at[:, pl.ds(g * SIG, SIG), :]
        return pltpu.make_async_copy(src, volts.at[g], load_sem.at[g])

    load(0).start()
    barrier = pltpu.get_barrier_semaphore()

    @pl.loop(1, n)
    def _(d):
        there = lax.rem(me + d, n)
        pl.semaphore_signal(barrier, inc=1, device_id={"st": there}, device_id_type=MESH)

    fill_slots(owner_ref, channel_ref, slots)
    fill_tables(slots, table)
    row = lax.broadcasted_iota(jnp.int32, (512, 2 * SLOTS), 0)
    col = lax.broadcasted_iota(jnp.int32, (512, 2 * SLOTS), 1)
    taken = ((row >> 3) & 1) * SLOTS + (row & 7) * 32 + (row >> 4)
    place[...] = ((taken == col) & ((row & 7) < PER_DEV)).astype(F32).astype(BF16)
    load(1).start()
    pl.semaphore_wait(barrier, n - 1)

    def own(q):
        return pltpu.make_async_copy(send.at[q, me], recv.at[q, me], own_sem.at[q])

    def remote(q, piece, there):
        rows = pl.ds(*PIECES[piece])
        return pltpu.make_async_remote_copy(
            src_ref=send.at[q, there, rows],
            dst_ref=recv.at[q, me, rows],
            send_sem=send_sem.at[q, piece],
            recv_sem=recv_sem.at[q, piece],
            device_id={"st": there},
            device_id_type=MESH,
        )

    def start(q, piece):
        plane, column, core = me // 8, (me // 2) % 4, me % 2
        for dz, dx, dc in ORDER:
            there = ((plane + dz) % 4) * 8 + ((column + dx) % 4) * 2 + (core + dc) % 2
            remote(q, piece, there).start()

    @pl.loop(0, 4)
    def _(step):
        g, half = step // 2, step % 2
        q = half * 2 + g

        @pl.when(half == 0)
        def _():
            src = volts_hbm.at[:, pl.ds(g * SIG, SIG), :]
            pltpu.make_async_copy(src, volts.at[g], load_sem.at[g]).wait()

        filter_frames(volts.at[g], half, proto_ref, filt, spec)

        def both(k1, which, rows):
            t = lax.dot_general(table[which, : 2 * rows], spec[k1], NT, preferred_element_type=F32)
            c, s = t[:rows], t[rows:]
            return c[:, :128] + s[:, 128:], c[:, 128:] - s[:, :128]

        chan = slots[0, :, 0:128].astype(jnp.int32)
        beam_re = jnp.zeros((SLOTS, 128), F32)
        beam_im = jnp.zeros((SLOTS, 128), F32)
        for k1 in range(4):
            re, im = both(k1, 4, SLOTS)
            mine = (chan & 3) == k1
            beam_re = jnp.where(mine, re, beam_re)
            beam_im = jnp.where(mine, im, beam_im)
        row = lax.broadcasted_iota(jnp.int32, (128, 128), 0)
        col = lax.broadcasted_iota(jnp.int32, (128, 128), 1)
        turn = (row == (col & 7) * 16 + (col >> 3)).astype(F32).astype(BF16)
        joined = jnp.concatenate([beam_re, beam_im], axis=0).astype(BF16)
        joined = jnp.dot(joined, turn, preferred_element_type=F32).astype(BF16)
        placed = jnp.dot(place[...], joined, preferred_element_type=F32)
        send[q, :, 0:16, :] = placed.astype(BF16).reshape(32, 16, 128)
        for k1 in range(4):
            re, im = both(k1, k1, 256)
            send[q, :, 16 + k1 * 16 : 32 + k1 * 16, :] = by_group(re, im)
            if k1 % 2 == 1:
                start(q, k1 // 2)
        own(q).start()

    @pl.loop(0, delay_ref.shape[0] // 32)
    def _(block):
        at = pl.ds(pl.multiple_of(block * 32, 32), 32)
        scaling = gain_ref[at, :] * (1.0 / math.sqrt(gain_ref.shape[1]))
        for slot in range(PER_DEV):
            mine = pl.ds(slot * 32 + me, 1)
            turns = delay_ref[at, :] * (slots[0, mine, :] * (1.0 / NCH))
            turns = turns - jnp.floor(turns)
            s, c = sincos_turns(turns)
            level = scaling * slots[1, mine, :]
            weight[slot, 0, at, :] = (level * c).astype(BF16)
            weight[slot, 1, at, :] = (-level * s).astype(BF16)

    copies = [pltpu.make_async_copy(weight, weight_hbm, out_sem.at[0])]
    copies[0].start()
    for g in range(2):
        for q in (g, 2 + g):
            own(q).wait()
            for piece in range(len(PIECES)):
                rows = pl.ds(*PIECES[piece])
                others = pl.ds(0, n - 1)
                all_of = pltpu.make_async_remote_copy(
                    src_ref=send.at[q, others, rows],
                    dst_ref=recv.at[q, others, rows],
                    send_sem=send_sem.at[q, piece],
                    recv_sem=recv_sem.at[q, piece],
                    device_id={"st": lax.rem(me + 1, n)},
                    device_id_type=MESH,
                )
                all_of.wait_send()
                all_of.wait_recv()
            beam = pltpu.make_async_copy(recv.at[q, :, 0:16], beam_hbm.at[q], out_sem.at[1 + q])
            beam.start()
            copies.append(beam)

        @pl.loop(0, n)
        def _(src):
            block = jnp.concatenate([recv[g, src, 16:80, :], recv[2 + g, src, 16:80, :]], axis=0)
            block = block.astype(F32)
            by_part = block.reshape(8, 2, 8, 128)
            swapped = jnp.stack([by_part[:, 1], -by_part[:, 0]], axis=1).reshape(128, 128)
            for x, dest in ((block, plain), (swapped, turned)):
                t = x.astype(BF16).T
                for f in range(HALF):
                    dest[src, g, :, f * 128 : f * 128 + 128] = t[f * SIG : f * SIG + SIG]

        for i, (mem, out) in enumerate(((plain, plain_hbm), (turned, turned_hbm))):
            copy = pltpu.make_async_copy(mem.at[:, g], out.at[:, g], out_sem.at[5 + 2 * g + i])
            copy.start()
            copies.append(copy)
    for copy in copies:
        copy.wait()


def exchange(volts, prototype, owners, channels, delays, gains):
    vmem = pl.BlockSpec(memory_space=pltpu.VMEM)
    hbm = pl.BlockSpec(memory_space=pl.ANY)
    blocks = (4, GROUPS, ROWS, 128)
    spectra = (GROUPS, 2, SIG, 1024)
    weight = (PER_DEV, 2) + delays.shape
    return pl.pallas_call(
        exchange_kernel,
        out_shape=[
            jax.ShapeDtypeStruct(spectra, BF16),
            jax.ShapeDtypeStruct(spectra, BF16),
            jax.ShapeDtypeStruct((4, GROUPS, 16, 128), BF16),
            jax.ShapeDtypeStruct(weight, BF16),
        ],
        in_specs=[hbm] + [vmem] * 5,
        out_specs=[hbm] * 4,
        scratch_shapes=[
            pltpu.VMEM((2, 2, SIG, volts.shape[2]), BF16),
            pltpu.VMEM((2, SLOTS, 256), F32),
            pltpu.VMEM((512, 2 * SLOTS), BF16),
            pltpu.VMEM((5, 512, QUARTER), BF16),
            pltpu.VMEM((8, HALF, SIG, 128), F32),
            pltpu.VMEM((4, 256, QUARTER), BF16),
            pltpu.VMEM(blocks, BF16),
            pltpu.VMEM(blocks, BF16),
            pltpu.VMEM(spectra, BF16),
            pltpu.VMEM(spectra, BF16),
            pltpu.VMEM(weight, BF16),
            pltpu.SemaphoreType.DMA((2,)),
            pltpu.SemaphoreType.DMA((4,)),
            pltpu.SemaphoreType.DMA((4, len(PIECES))),
            pltpu.SemaphoreType.DMA((4, len(PIECES))),
            pltpu.SemaphoreType.DMA((9,)),
        ],
        compiler_params=pltpu.CompilerParams(
            vmem_limit_bytes=VMEM_LIMIT, collective_id=0, has_side_effects=True
        ),
        name="exchange",
    )(volts, prototype, owners, channels, delays, gains)


def correlate_kernel(plain_ref, turned_ref, beam_ref, weight_ref, station_ref, vis_ref, beam_out_ref, wide):
    @pl.when(pl.program_id(0) == 0)
    def _():
        listed = station_ref.shape[1]
        row = lax.broadcasted_iota(jnp.int32, (512, listed), 0)
        station = (row & 31) * 16 + ((row >> 5) & 1) * 8 + (row >> 6)
        select = (station == station_ref[...]).astype(F32).astype(BF16)
        wide[...] = beam_ref[...].reshape(4 * 512, 128).astype(F32)
        rows = []
        for slot in range(PER_DEV):
            for part in range(2):
                for half in range(2):
                    first = half * 1024 + part * 8 + slot
                    x = wide[pl.ds(first, 64, stride=16), :]
                    t = x.T.astype(BF16)
                    rows.append(jnp.concatenate([t[s * 16 : s * 16 + 16] for s in range(8)], axis=1))
        picked = jnp.dot(jnp.concatenate(rows, axis=0), select, preferred_element_type=F32).astype(BF16)
        for slot in range(PER_DEV):
            pair = picked[slot * 64 : slot * 64 + 64]
            with_re = lax.dot_general(pair, weight_ref[slot, 0], NT, preferred_element_type=F32)
            with_im = lax.dot_general(pair, weight_ref[slot, 1], NT, preferred_element_type=F32)
            out_re = with_re[:32] - with_im[32:]
            out_im = with_re[32:] + with_im[:32]
            for part, out in enumerate((out_re, out_im)):
                for half in range(2):
                    for p in range(2):
                        at = half * 16 + p * 8
                        lanes = slice(p * 256, p * 256 + 256)
                        beam_out_ref[0, slot, part, half * 8 : half * 8 + 8, lanes] = out[at : at + 8]

    cols = pl.ds(pl.multiple_of(pl.program_id(0) * 256, 256), 256)
    scale = 1.0 / 512
    for part, left in enumerate((plain_ref, turned_ref)):
        total = lax.dot_general(left[...], plain_ref[cols, :], NT, preferred_element_type=F32)
        vis_ref[part, 0, 0] = total * scale


def correlate(plain, turned, beam, weight, station_index):
    once = pl.Buffered(1)

    def whole(x):
        zeros = (0,) * len(x.shape)
        return pl.BlockSpec(x.shape, lambda i: zeros, pipeline_mode=once)

    beam_out = jax.ShapeDtypeStruct((1, PER_DEV, 2, FRAMES, 512), F32)
    operands = (plain, turned, beam, weight, station_index)
    return pl.pallas_call(
        correlate_kernel,
        grid=(4,),
        out_shape=[jax.ShapeDtypeStruct((2, 1, 1, SIGNALS, SIGNALS), F32), beam_out],
        in_specs=[whole(x) for x in operands],
        out_specs=[
            pl.BlockSpec((2, 1, 1, SIGNALS, 256), lambda i: (0, 0, 0, 0, i)),
            whole(beam_out),
        ],
        scratch_shapes=[pltpu.VMEM((2048, 128), F32)],
        compiler_params=pltpu.CompilerParams(vmem_limit_bytes=VMEM_LIMIT),
        name="correlate",
    )(*operands)


def body(volts, prototype, beam_channels, station_index, delays, gains, assign):
    owners = assign.reshape(1, -1)
    plain, turned, beam, weight = exchange(volts, prototype, owners, beam_channels, delays, gains)
    rows = (SIGNALS, 1024)
    return tuple(correlate(plain.reshape(rows), turned.reshape(rows), beam, weight, station_index[None]))


def solution(mesh):
    in_specs = (P(None, "st", None), P(), P(), P(), P(), P(), P())
    out_specs = (P(None, "sb", "st", None, None), P("sb", "st", None, None, None))
    return jax.shard_map(body, mesh=mesh, in_specs=in_specs, out_specs=out_specs, check_vma=False)
```

```python
import math

import jax
import jax.numpy as jnp
from jax import lax
from jax.experimental import pallas as pl
from jax.experimental.pallas import tpu as pltpu
from jax.sharding import PartitionSpec as P

NCH = 4096
FRAMES = 16
TAPS = 16
SLOTS = 160
BAND = 1024
GROUPS = 32
PER_DEV = 5
QUARTER = 1024
SIG = 16
SIGNALS = 1024
ROWS = 80
NT = (((1,), (1,)), ((), ()))
F32 = jnp.float32
BF16 = jnp.bfloat16
VMEM_LIMIT = 56 << 20
MESH = pl.DeviceIdType.MESH
PIECES = ((0, 32), (32, 48))
HALF = 8
CHIPS = ((2, 2), (1, 2), (2, 1), (3, 2), (2, 3), (0, 2), (2, 0), (1, 1), (3, 3), (1, 3), (3, 1), (0, 1), (3, 0), (0, 3), (1, 0))
ORDER = tuple((z, x, c) for z, x in CHIPS for c in range(2)) + ((0, 0, 1),)


def sincos_turns(turns):
    quarter = jnp.floor(turns * 4.0 + 0.5)
    x = (turns - quarter * 0.25) * (2.0 * math.pi)
    z = x * x
    sin_x = x * (1.0 + z * (-1.0 / 6 + z * (1.0 / 120 + z * (-1.0 / 5040 + z * (1.0 / 362880)))))
    cos_x = 1.0 + z * (-0.5 + z * (1.0 / 24 + z * (-1.0 / 720 + z * (1.0 / 40320))))
    which = quarter.astype(jnp.int32) & 3
    odd = (which & 1) == 1
    s = jnp.where(odd, cos_x, sin_x)
    c = jnp.where(odd, sin_x, cos_x)
    s = jnp.where(which >= 2, -s, s)
    c = jnp.where((which == 1) | (which == 2), -c, c)
    return s, c


def fill_slots(owner_ref, channel_ref, slots):
    entries = owner_ref.shape[1]
    match = owner_ref[...] == lax.axis_index("sb")
    ones = jnp.broadcast_to(match.astype(F32), (8, entries)).astype(BF16)
    row = lax.broadcasted_iota(jnp.int32, (entries, entries), 0)
    col = lax.broadcasted_iota(jnp.int32, (entries, entries), 1)
    earlier = (row < col).astype(F32).astype(BF16)
    position = jnp.dot(ones, earlier, preferred_element_type=F32)[0:1].astype(jnp.int32)
    position = jnp.where(match, position, -1)
    line = lax.broadcasted_iota(jnp.int32, (SLOTS, entries), 0)
    pick = (position == (line & 31) * PER_DEV + (line >> 5)).astype(F32)
    chan = jnp.sum(pick * channel_ref[...].reshape(1, entries).astype(F32), axis=1, keepdims=True)
    filled = jnp.sum(pick, axis=1, keepdims=True)
    slots[0] = jnp.broadcast_to(chan, (SLOTS, 256))
    slots[1] = jnp.broadcast_to(filled, (SLOTS, 256))


def fill_tables(slots, table):
    def fill(wide, which, cos_row, sin_row):
        lane = lax.broadcasted_iota(jnp.int32, (32, 128), 1)
        s, c = sincos_turns(((lane * wide) & (NCH - 1)).astype(F32) * (1.0 / NCH))
        s_step, c_step = sincos_turns(((128 * wide) & (NCH - 1)).astype(F32) * (1.0 / NCH))
        s, c = s * (1.0 / 64), c * (1.0 / 64)
        cos_at = pl.ds(pl.multiple_of(cos_row, 32), 32)
        sin_at = pl.ds(pl.multiple_of(sin_row, 32), 32)
        for tile in range(QUARTER // 128):
            lanes = slice(tile * 128, tile * 128 + 128)
            table[which, cos_at, lanes] = c.astype(BF16)
            table[which, sin_at, lanes] = s.astype(BF16)
            s, c = s * c_step + c * s_step, c * c_step - s * s_step

    first = lax.axis_index("sb") * BAND

    @pl.loop(0, 32)
    def _(block):
        k1, row = block // 8, (block % 8) * 32
        line = lax.broadcasted_iota(jnp.int32, (32, 128), 0)
        fill(first + (row + line) * 4 + k1, k1, row, row + 256)

    @pl.loop(0, SLOTS // 32)
    def _(block):
        rows = pl.ds(pl.multiple_of(block * 32, 32), 32)
        fill(slots[0, rows, 0:128].astype(jnp.int32), 4, block * 32, block * 32 + SLOTS)


def filter_frames(volts, half, proto_ref, filt, spec):
    @pl.loop(0, QUARTER // 128)
    def _(tile):
        @pl.loop(0, 4)
        def _(n1):
            base = pl.multiple_of(n1 * QUARTER + tile * 128, 128)
            taps = [
                jnp.broadcast_to(proto_ref[t : t + 1, pl.ds(base, 128)], (8, 128))
                for t in range(TAPS)
            ]
            h0, h1 = taps[0::2], taps[1::2]
            hd = [b - a for a, b in zip(h0, h1)]
            for part in range(2):
                for rows in (slice(0, 8), slice(8, 16)):

                    def frame(u):
                        at = pl.multiple_of((half * HALF + u) * NCH + base, 128)
                        return volts[part, rows, pl.ds(at, 128)].astype(F32)

                    acc = [[None] * (HALF // 2) for _ in range(3)]
                    x0 = frame(0)
                    for j in range((HALF + TAPS) // 2 - 1):
                        x1, after = frame(2 * j + 1), frame(2 * j + 2)
                        terms = ((hd, x1), (h0, x0 + x1), (h1, x1 + after))
                        for m in range(HALF // 2):
                            i = j - m
                            if 0 <= i < TAPS // 2:
                                for total, (h, x) in zip(acc, terms):
                                    total[m] = h[i] * x if total[m] is None else total[m] + h[i] * x
                        x0 = after
                    for m in range(HALF // 2):
                        filt[part * 4 + n1, 2 * m, rows] = acc[1][m] + acc[0][m]
                        filt[part * 4 + n1, 2 * m + 1, rows] = acc[2][m] - acc[0][m]

        lanes = pl.ds(pl.multiple_of(tile * 128, 128), 128)
        for f in range(HALF):
            re = [filt[n1, f] for n1 in range(4)]
            im = [filt[4 + n1, f] for n1 in range(4)]
            ar, ai = re[0] + re[2], im[0] + im[2]
            br, bi = re[0] - re[2], im[0] - im[2]
            cr, ci = re[1] + re[3], im[1] + im[3]
            dr, di = re[1] - re[3], im[1] - im[3]
            outs = [(ar + cr, ai + ci), (br + di, bi - dr), (ar - cr, ai - ci), (br - di, bi + dr)]
            for k1 in range(4):
                for part in range(2):
                    at = part * 128 + f * SIG
                    spec[k1, at : at + SIG, lanes] = outs[k1][part].astype(BF16)


def by_group(re, im):
    joined = jnp.concatenate([re.reshape(32, 8, 128), im.reshape(32, 8, 128)], axis=1)
    return joined.astype(BF16)


def exchange_kernel(
    volts_hbm, proto_ref, owner_ref, channel_ref, delay_ref, gain_ref,
    plain_hbm, turned_hbm, beam_hbm, weight_hbm,
    volts, slots, place, table, filt, spec, send, recv, plain, turned, weight,
    load_sem, own_sem, send_sem, recv_sem, out_sem,
):
    n = GROUPS
    me = lax.axis_index("st")

    def load(g):
        src = volts_hbm.at[:, pl.ds(g * SIG, SIG), :]
        return pltpu.make_async_copy(src, volts.at[g], load_sem.at[g])

    load(0).start()
    barrier = pltpu.get_barrier_semaphore()

    @pl.loop(1, n)
    def _(d):
        there = lax.rem(me + d, n)
        pl.semaphore_signal(barrier, inc=1, device_id={"st": there}, device_id_type=MESH)

    fill_slots(owner_ref, channel_ref, slots)
    fill_tables(slots, table)
    row = lax.broadcasted_iota(jnp.int32, (512, 2 * SLOTS), 0)
    col = lax.broadcasted_iota(jnp.int32, (512, 2 * SLOTS), 1)
    taken = ((row >> 3) & 1) * SLOTS + (row & 7) * 32 + (row >> 4)
    place[...] = ((taken == col) & ((row & 7) < PER_DEV)).astype(F32).astype(BF16)
    load(1).start()
    pl.semaphore_wait(barrier, n - 1)

    def own(q):
        return pltpu.make_async_copy(send.at[q, me], recv.at[q, me], own_sem.at[q])

    def remote(q, piece, there):
        rows = pl.ds(*PIECES[piece])
        return pltpu.make_async_remote_copy(
            src_ref=send.at[q, there, rows],
            dst_ref=recv.at[q, me, rows],
            send_sem=send_sem.at[q, piece],
            recv_sem=recv_sem.at[q, piece],
            device_id={"st": there},
            device_id_type=MESH,
        )

    def start(q, piece):
        plane, column, core = me // 8, (me // 2) % 4, me % 2
        for dz, dx, dc in ORDER:
            there = ((plane + dz) % 4) * 8 + ((column + dx) % 4) * 2 + (core + dc) % 2
            remote(q, piece, there).start()

    @pl.loop(0, 4)
    def _(step):
        g, half = step // 2, step % 2
        q = half * 2 + g

        @pl.when(half == 0)
        def _():
            src = volts_hbm.at[:, pl.ds(g * SIG, SIG), :]
            pltpu.make_async_copy(src, volts.at[g], load_sem.at[g]).wait()

        filter_frames(volts.at[g], half, proto_ref, filt, spec)

        def both(k1, which, rows):
            t = lax.dot_general(table[which, : 2 * rows], spec[k1], NT, preferred_element_type=F32)
            c, s = t[:rows], t[rows:]
            return c[:, :128] + s[:, 128:], c[:, 128:] - s[:, :128]

        for k1 in range(4):
            re, im = both(k1, k1, 256)
            send[q, :, k1 * 16 : k1 * 16 + 16, :] = by_group(re, im)
            if k1 == 1:
                start(q, 0)
        chan = slots[0, :, 0:128].astype(jnp.int32)
        beam_re = jnp.zeros((SLOTS, 128), F32)
        beam_im = jnp.zeros((SLOTS, 128), F32)
        for k1 in range(4):
            re, im = both(k1, 4, SLOTS)
            mine = (chan & 3) == k1
            beam_re = jnp.where(mine, re, beam_re)
            beam_im = jnp.where(mine, im, beam_im)
        row = lax.broadcasted_iota(jnp.int32, (128, 128), 0)
        col = lax.broadcasted_iota(jnp.int32, (128, 128), 1)
        turn = (row == (col & 7) * 16 + (col >> 3)).astype(F32).astype(BF16)
        joined = jnp.concatenate([beam_re, beam_im], axis=0).astype(BF16)
        joined = jnp.dot(joined, turn, preferred_element_type=F32).astype(BF16)
        placed = jnp.dot(place[...], joined, preferred_element_type=F32)
        send[q, :, 64:80, :] = placed.astype(BF16).reshape(32, 16, 128)
        start(q, 1)
        own(q).start()

    @pl.loop(0, delay_ref.shape[0] // 32)
    def _(block):
        at = pl.ds(pl.multiple_of(block * 32, 32), 32)
        scaling = gain_ref[at, :] * (1.0 / math.sqrt(gain_ref.shape[1]))
        for slot in range(PER_DEV):
            mine = pl.ds(slot * 32 + me, 1)
            turns = delay_ref[at, :] * (slots[0, mine, :] * (1.0 / NCH))
            turns = turns - jnp.floor(turns)
            s, c = sincos_turns(turns)
            level = scaling * slots[1, mine, :]
            weight[slot, 0, at, :] = (level * c).astype(BF16)
            weight[slot, 1, at, :] = (-level * s).astype(BF16)

    copies = [pltpu.make_async_copy(weight, weight_hbm, out_sem.at[0])]
    copies[0].start()
    for g in range(2):
        for q in (g, 2 + g):
            own(q).wait()
            for piece in range(len(PIECES)):
                rows = pl.ds(*PIECES[piece])
                others = pl.ds(0, n - 1)
                all_of = pltpu.make_async_remote_copy(
                    src_ref=send.at[q, others, rows],
                    dst_ref=recv.at[q, others, rows],
                    send_sem=send_sem.at[q, piece],
                    recv_sem=recv_sem.at[q, piece],
                    device_id={"st": lax.rem(me + 1, n)},
                    device_id_type=MESH,
                )
                all_of.wait_send()
                all_of.wait_recv()
            beam = pltpu.make_async_copy(recv.at[q, :, 64:80], beam_hbm.at[q], out_sem.at[1 + q])
            beam.start()
            copies.append(beam)

        @pl.loop(0, n)
        def _(src):
            block = jnp.concatenate([recv[g, src, 0:64, :], recv[2 + g, src, 0:64, :]], axis=0)
            block = block.astype(F32)
            by_part = block.reshape(8, 2, 8, 128)
            swapped = jnp.stack([by_part[:, 1], -by_part[:, 0]], axis=1).reshape(128, 128)
            for x, dest in ((block, plain), (swapped, turned)):
                t = x.astype(BF16).T
                for f in range(HALF):
                    dest[src, g, :, f * 128 : f * 128 + 128] = t[f * SIG : f * SIG + SIG]

        for i, (mem, out) in enumerate(((plain, plain_hbm), (turned, turned_hbm))):
            copy = pltpu.make_async_copy(mem.at[:, g], out.at[:, g], out_sem.at[5 + 2 * g + i])
            copy.start()
            copies.append(copy)
    for copy in copies:
        copy.wait()


def exchange(volts, prototype, owners, channels, delays, gains):
    vmem = pl.BlockSpec(memory_space=pltpu.VMEM)
    hbm = pl.BlockSpec(memory_space=pl.ANY)
    blocks = (4, GROUPS, ROWS, 128)
    spectra = (GROUPS, 2, SIG, 1024)
    weight = (PER_DEV, 2) + delays.shape
    return pl.pallas_call(
        exchange_kernel,
        out_shape=[
            jax.ShapeDtypeStruct(spectra, BF16),
            jax.ShapeDtypeStruct(spectra, BF16),
            jax.ShapeDtypeStruct((4, GROUPS, 16, 128), BF16),
            jax.ShapeDtypeStruct(weight, BF16),
        ],
        in_specs=[hbm] + [vmem] * 5,
        out_specs=[hbm] * 4,
        scratch_shapes=[
            pltpu.VMEM((2, 2, SIG, volts.shape[2]), BF16),
            pltpu.VMEM((2, SLOTS, 256), F32),
            pltpu.VMEM((512, 2 * SLOTS), BF16),
            pltpu.VMEM((5, 512, QUARTER), BF16),
            pltpu.VMEM((8, HALF, SIG, 128), F32),
            pltpu.VMEM((4, 256, QUARTER), BF16),
            pltpu.VMEM(blocks, BF16),
            pltpu.VMEM(blocks, BF16),
            pltpu.VMEM(spectra, BF16),
            pltpu.VMEM(spectra, BF16),
            pltpu.VMEM(weight, BF16),
            pltpu.SemaphoreType.DMA((2,)),
            pltpu.SemaphoreType.DMA((4,)),
            pltpu.SemaphoreType.DMA((4, len(PIECES))),
            pltpu.SemaphoreType.DMA((4, len(PIECES))),
            pltpu.SemaphoreType.DMA((9,)),
        ],
        compiler_params=pltpu.CompilerParams(
            vmem_limit_bytes=VMEM_LIMIT, collective_id=0, has_side_effects=True
        ),
        name="exchange",
    )(volts, prototype, owners, channels, delays, gains)


def correlate_kernel(plain_ref, turned_ref, beam_ref, weight_ref, station_ref, vis_ref, beam_out_ref, wide):
    @pl.when(pl.program_id(0) == 0)
    def _():
        listed = station_ref.shape[1]
        row = lax.broadcasted_iota(jnp.int32, (512, listed), 0)
        station = (row & 31) * 16 + ((row >> 5) & 1) * 8 + (row >> 6)
        select = (station == station_ref[...]).astype(F32).astype(BF16)
        wide[...] = beam_ref[...].reshape(4 * 512, 128).astype(F32)
        rows = []
        for slot in range(PER_DEV):
            for part in range(2):
                for half in range(2):
                    first = half * 1024 + part * 8 + slot
                    x = wide[pl.ds(first, 64, stride=16), :]
                    t = x.T.astype(BF16)
                    rows.append(jnp.concatenate([t[s * 16 : s * 16 + 16] for s in range(8)], axis=1))
        picked = jnp.dot(jnp.concatenate(rows, axis=0), select, preferred_element_type=F32).astype(BF16)
        for slot in range(PER_DEV):
            pair = picked[slot * 64 : slot * 64 + 64]
            with_re = lax.dot_general(pair, weight_ref[slot, 0], NT, preferred_element_type=F32)
            with_im = lax.dot_general(pair, weight_ref[slot, 1], NT, preferred_element_type=F32)
            out_re = with_re[:32] - with_im[32:]
            out_im = with_re[32:] + with_im[:32]
            for part, out in enumerate((out_re, out_im)):
                for half in range(2):
                    for p in range(2):
                        at = half * 16 + p * 8
                        lanes = slice(p * 256, p * 256 + 256)
                        beam_out_ref[0, slot, part, half * 8 : half * 8 + 8, lanes] = out[at : at + 8]

    cols = pl.ds(pl.multiple_of(pl.program_id(0) * 256, 256), 256)
    scale = 1.0 / 512
    for part, left in enumerate((plain_ref, turned_ref)):
        total = lax.dot_general(left[...], plain_ref[cols, :], NT, preferred_element_type=F32)
        vis_ref[part, 0, 0] = total * scale


def correlate(plain, turned, beam, weight, station_index):
    once = pl.Buffered(1)

    def whole(x):
        zeros = (0,) * len(x.shape)
        return pl.BlockSpec(x.shape, lambda i: zeros, pipeline_mode=once)

    beam_out = jax.ShapeDtypeStruct((1, PER_DEV, 2, FRAMES, 512), F32)
    operands = (plain, turned, beam, weight, station_index)
    return pl.pallas_call(
        correlate_kernel,
        grid=(4,),
        out_shape=[jax.ShapeDtypeStruct((2, 1, 1, SIGNALS, SIGNALS), F32), beam_out],
        in_specs=[whole(x) for x in operands],
        out_specs=[
            pl.BlockSpec((2, 1, 1, SIGNALS, 256), lambda i: (0, 0, 0, 0, i)),
            whole(beam_out),
        ],
        scratch_shapes=[pltpu.VMEM((2048, 128), F32)],
        compiler_params=pltpu.CompilerParams(vmem_limit_bytes=VMEM_LIMIT),
        name="correlate",
    )(*operands)


def body(volts, prototype, beam_channels, station_index, delays, gains, assign):
    owners = assign.reshape(1, -1)
    plain, turned, beam, weight = exchange(volts, prototype, owners, beam_channels, delays, gains)
    rows = (SIGNALS, 1024)
    return tuple(correlate(plain.reshape(rows), turned.reshape(rows), beam, weight, station_index[None]))


def solution(mesh):
    in_specs = (P(None, "st", None), P(), P(), P(), P(), P(), P())
    out_specs = (P(None, "sb", "st", None, None), P("sb", "st", None, None, None))
    return jax.shard_map(body, mesh=mesh, in_specs=in_specs, out_specs=out_specs, check_vma=False)
```
